128 devices in a mesh: row: 16 (over y, x), col: 8 (over z, core).
Axes of the slice: x: 4, y: 4, z: 4, core: 2. Of those that a mesh axis runs over, the one named last changes fastest.
Arguments:
- snapshots: float32 [65536, 2048], P(('row', 'col')), may hold values from -6 to 6
- district: int32 [65536], P(('row', 'col')), may hold values from 0 to 255, never falling along the last dimension, each value on 1 to 1024 neighbouring positions
- target: int32 [65536], replicated, may hold values from 0 to 65535, as said below
Outputs:
- coefficients: float32 [512, 2048], P(None, 'col')
- remainder: float32 [65536, 2048], P('row', 'col')
The draws below stay inside these ranges and needn't reach their ends.
Inputs may be any that keep to these rules, and one draw needn't show every extreme that they name: A permutation of the storage rows; each aligned block of 512 nodes has exactly 512 / 16 nodes whose target lies in each aligned block of 4096 storage rows. `district`: districts never fall along the nodes, and each holds at most 1024 nodes.
All inputs are finite; a program needn't handle non-finite values.
Results may differ from the reference program's by a relative error of at most 0.0001.
Values sent between devices are 32-bit elements; how exact they have to be, the bound alone decides.
A program may use at most 128 MiB of HBM per device.

```python
import math
import jax
import jax.numpy as jnp
import numpy as np
from jax import lax

NODES_DEV = 512
SNAPS = 2048
NB = 256
DIST_MEAN = 256
NODES = 65536
NDIST = 256
LOC = 4096
SOURCES = 128
N_COL = 8


def draw_target(key, part):
    first_key, second_key = jax.random.split(key)
    owners = NODES // LOC
    per_owner = NODES_DEV // owners
    owner_keys = jax.random.split(first_key, owners)
    slots = jax.vmap(lambda single: jax.random.permutation(single, LOC))(owner_keys)
    slots = slots.reshape(owners, SOURCES, per_owner)
    placed = jnp.arange(owners, dtype=jnp.int32)[:, None, None] * LOC + slots.astype(jnp.int32)
    by_source = placed.transpose(1, 0, 2).reshape(SOURCES, NODES_DEV)
    source_keys = jax.random.split(second_key, SOURCES)
    shuffle = jax.vmap(lambda single: jax.random.permutation(single, NODES_DEV))(source_keys)
    result = jnp.take_along_axis(by_source, shuffle.astype(jnp.int32), axis=1)
    return result.reshape(NODES).astype(jnp.int32)


def block_levels(own_key, dims, cuts, smallest, largest):
    def one(position, blocks):
        steps = jax.random.uniform(jax.random.fold_in(jax.random.fold_in(own_key, 6), position), (blocks,), jnp.float32, smallest / len(cuts), largest / len(cuts))
        return jnp.repeat(jnp.exp(steps), dims[position] // blocks).reshape((-1,) + (1,) * (len(dims) - position - 1))

    gain = one(*cuts[0])
    for cut in cuts[1:]:
        gain = gain * one(*cut)
    return gain


def length_profile(number_of, total, bound, slope):
    weights = [(1 << 20) // math.isqrt(standing ** slope) + 1 for standing in range(2, number_of + 1)]
    rest, given = total - bound - (number_of - 1), [1] * (number_of - 1)
    while rest > 0:
        candidates = [i for i in range(number_of - 1) if given[i] < bound]
        pool, remaining = sum([weights[i] for i in candidates]), rest
        for i in candidates:
            more = min(bound - given[i], max(1, remaining * weights[i] // pool), rest)
            given[i] = given[i] + more
            rest = rest - more
    return np.array([bound] + given)


def uneven_parts(own_key, number_of, total, most, slope):
    if number_of == 2:
        one = jax.random.randint(own_key, (), max(1, total - most), min(most, total - 1) + 1)
        return jnp.stack([one, total - one])
    sizes = jnp.asarray(length_profile(number_of, total, most, slope), jnp.int32)
    couples = (number_of - 1) // 2
    giver, receiver = sizes[1:1 + 2 * couples:2], sizes[2:2 + 2 * couples:2]
    room = jnp.minimum(giver - 1, most - receiver)
    shifted = jax.random.randint(jax.random.fold_in(own_key, 1), (couples,), 0, 1 << 20) % (room + 1)
    sizes = sizes.at[1:1 + 2 * couples:2].set(giver - shifted).at[2:2 + 2 * couples:2].set(receiver + shifted)
    return sizes[jax.random.permutation(jax.random.fold_in(own_key, 2), number_of)]


def bell_draw(own_key, extent, scale, limit, shards=(), kind=jnp.bfloat16):
    drawn = scale * jax.random.normal(own_key, extent, jnp.float32)
    if shards:
        drawn = drawn * block_levels(own_key, extent, shards, -0.22, 0.18)
    return jnp.clip(drawn, -limit, limit).astype(kind)


def setup_inputs(seed: int = 0) -> dict:
    splits = jax.random.split(jax.random.key(seed), 4)
    snapshots = bell_draw(splits[0], (NODES, SNAPS), 1.0, 6.0, ((0, 128),), jnp.float32)
    district = jnp.searchsorted(jnp.cumsum(uneven_parts(splits[1], NDIST, NODES, 4 * DIST_MEAN, 2)), jnp.arange(NODES), side="right").astype(jnp.int32)
    target = draw_target(jax.random.fold_in(splits[3], 71), 0)
    return dict(snapshots=snapshots, district=district, target=target)


HIGH = lax.Precision.HIGHEST

def orthonormal(panel, gram):
    lower = jnp.linalg.cholesky(gram)
    inverse = jax.scipy.linalg.solve_triangular(lower, jnp.eye(gram.shape[0], dtype=gram.dtype), lower=True)
    return jnp.dot(panel, inverse.T, precision=HIGH)

def reference(snapshots, district, target):
    nodes = snapshots.shape[0]
    counts = jax.ops.segment_sum(jnp.ones((nodes,), jnp.float32), district, num_segments=NDIST)
    scale = jnp.sqrt(DIST_MEAN / jnp.maximum(counts, 1.0))
    weighted = snapshots * scale[district][:, None]
    grid = jnp.zeros((nodes, SNAPS), jnp.float32).at[target].set(weighted)
    grid = grid.reshape(nodes, SNAPS // (NB * N_COL), N_COL, NB).transpose(0, 2, 1, 3).reshape(nodes, SNAPS)
    stacked = []
    for panel_index in range(2):
        start = panel_index % N_COL * (SNAPS // N_COL) + panel_index // N_COL * NB
        panel = grid[:, start:start + NB]
        gram = jnp.dot(panel.T, panel, precision=HIGH)
        basis = orthonormal(panel, gram)
        projection = jnp.dot(basis.T, grid, precision=HIGH)
        grid = grid - jnp.dot(basis, projection, precision=HIGH)
        stacked.append(projection)
    return (jnp.concatenate(stacked, axis=0), grid)
```

```python
import jax
import jax.numpy as jnp
from jax import lax
from jax.experimental import pallas as pl
from jax.experimental.pallas import tpu as pltpu
from jax.sharding import PartitionSpec as P

MESH = pl.DeviceIdType.MESH
NB = 256
PANELS = 2
K = PANELS * NB
DIST_MEAN = 256
HIGH = lax.Precision.HIGHEST
F32 = jnp.float32
BF16 = jnp.bfloat16
VMEM = pl.BlockSpec(memory_space=pltpu.VMEM)


def split2(x):
    hi = x.astype(BF16)
    return hi, (x - hi.astype(F32)).astype(BF16)


def dims(a, b):
    return (((a,), (b,)), ((), ()))


def mm(x, y, a=1, b=0):
    return lax.dot_general(x, y, dims(a, b), preferred_element_type=F32)


def mm3(xh, xl, yh, yl, a=1, b=0):
    return mm(xh, yh, a, b) + (mm(xh, yl, a, b) + mm(xl, yh, a, b))


def counts_kernel(district_ref, weight_ref, own, got, send_sem, recv_sem):
    row, col = lax.axis_index("row"), lax.axis_index("col")
    n_row, n_col = lax.axis_size("row"), lax.axis_size("col")
    n = n_row * n_col
    me = row * n_col + col
    steps = (n - 2, n - 1, 1, 2)

    def peer(step):
        other = lax.rem(me + step, n)
        return other // n_col, lax.rem(other, n_col)

    barrier = pltpu.get_barrier_semaphore()
    for step in steps:
        pl.semaphore_signal(barrier, inc=1, device_id=peer(step), device_id_type=MESH)
    nodes = district_ref.shape[0]
    lanes = lax.broadcasted_iota(jnp.int32, (nodes, 256), 1)
    member = district_ref[...] == lanes
    hist = jnp.sum(jnp.where(member, 1.0, 0.0), axis=0, keepdims=True)
    own[...] = jnp.broadcast_to(hist, own.shape)
    pl.semaphore_wait(barrier, 4)
    copies = []
    for k, step in enumerate(steps):
        copy = pltpu.make_async_remote_copy(
            own, got.at[k], send_sem.at[k], recv_sem.at[k], device_id=peer(step), device_id_type=MESH
        )
        copy.start()
        copies.append(copy)
    for copy in copies:
        copy.wait()
    total = own[...]
    valid = (me + 2 < n, me + 1 < n, me >= 1, me >= 2)
    for k in range(4):
        total = total + got[k] * jnp.where(valid[k], 1.0, 0.0)
    scale = jnp.sqrt(DIST_MEAN / jnp.maximum(total, 1.0))[0:1, :]
    weight_ref[...] = jnp.sum(jnp.where(member, scale, 0.0), axis=1, keepdims=True)


def weights_of(district):
    nodes = district.shape[0]
    return pl.pallas_call(
        counts_kernel,
        out_shape=jax.ShapeDtypeStruct((nodes, 1), F32),
        in_specs=[VMEM],
        out_specs=VMEM,
        scratch_shapes=[
            pltpu.VMEM((8, 256), F32),
            pltpu.VMEM((4, 8, 256), F32),
            pltpu.SemaphoreType.DMA((4,)),
            pltpu.SemaphoreType.DMA((4,)),
        ],
        compiler_params=pltpu.CompilerParams(collective_id=0, has_side_effects=True),
        name="counts",
    )(district.reshape(nodes, 1))


def prep_kernel(local_rows, n_row, panel_ref, x_ref, weight_ref, target_ref, rows_ref, gram_ref, left_hi, left_lo, perm):
    nodes = x_ref.shape[0]
    per = nodes // n_row

    @pl.when(pl.program_id(0) == 0)
    def _():
        left = panel_ref[...] * weight_ref[...]
        hi, lo = split2(left)
        left_hi[...] = hi.T
        left_lo[...] = lo.T
        owner = target_ref[...] // local_rows
        groups = lax.broadcasted_iota(jnp.int32, (n_row, nodes), 0)
        mask = jnp.where(owner == groups, 1.0, 0.0)
        before = jnp.where(
            lax.broadcasted_iota(jnp.int32, (nodes, nodes), 0) < lax.broadcasted_iota(jnp.int32, (nodes, nodes), 1), 1.0, 0.0
        ).astype(BF16)
        rank = mm(mask.astype(BF16), before)
        base = groups.astype(F32) * per
        place = jnp.sum(mask * (rank + base), axis=0, keepdims=True).astype(jnp.int32)
        perm[...] = jnp.where(place == lax.broadcasted_iota(jnp.int32, (nodes, nodes), 0), 1.0, 0.0).astype(BF16)

    x = x_ref[...] * weight_ref[...]
    hi = x.astype(BF16)
    rest = x - hi.astype(F32)
    mid = rest.astype(BF16)
    low = (rest - mid.astype(F32)).astype(BF16)
    p = perm[...]
    rows_ref[...] = (mm(p, hi) + mm(p, mid)) + mm(p, low)
    gram_ref[...] = mm3(left_hi[...], left_lo[...], hi, mid)


def prep(snapshots, weight, mine, n_row, local_rows):
    nodes, snaps = snapshots.shape
    out = jax.ShapeDtypeStruct((nodes, snaps), F32), jax.ShapeDtypeStruct((K, snaps), F32)
    return pl.pallas_call(
        lambda *refs: prep_kernel(local_rows, n_row, *refs),
        grid=(snaps // NB,),
        out_shape=out,
        in_specs=[
            pl.BlockSpec((nodes, K), lambda i: (0, 0)),
            pl.BlockSpec((nodes, NB), lambda i: (0, i)),
            pl.BlockSpec((nodes, 1), lambda i: (0, 0)),
            pl.BlockSpec((1, nodes), lambda i: (0, 0)),
        ],
        out_specs=(pl.BlockSpec((nodes, NB), lambda i: (0, i)), pl.BlockSpec((K, NB), lambda i: (0, i))),
        scratch_shapes=[pltpu.VMEM((K, nodes), BF16), pltpu.VMEM((K, nodes), BF16), pltpu.VMEM((nodes, nodes), BF16)],
        compiler_params=pltpu.CompilerParams(vmem_limit_bytes=32 << 20),
        name="prep",
    )(snapshots, snapshots, weight, mine.reshape(1, nodes))


def sum_kernel(a_ref, out_ref, acc, got0, got1, got2, got3, send_sem, recv_sem):
    row, col = lax.axis_index("row"), lax.axis_index("col")
    y, x, z, core = row // 4, lax.rem(row, 4), col // 2, lax.rem(col, 2)
    half = a_ref.shape[0] // 2
    q1, q2 = half // 4, half // 16
    width = a_ref.shape[1] // 4
    first = (1 - core) * x + core * y
    second = (1 - core) * y + core * x

    def pair(p, q):
        return ((1 - core) * q + core * p) * 4 + (1 - core) * p + core * q

    def peer1(d):
        return pair(lax.rem(first + d, 4), second), col

    def peer2(d):
        return pair(first, lax.rem(second + d, 4)), col

    def peer3(d):
        return row, lax.rem(z + d, 4) * 2 + core

    sibling = (row, z * 2 + 1 - core)
    barrier = pltpu.get_barrier_semaphore()
    everyone = [sibling] + [peer(d) for peer in (peer1, peer2, peer3) for d in (1, 2, 3)]
    for one in everyone:
        pl.semaphore_signal(barrier, inc=1, device_id=one, device_id_type=MESH)
    pl.semaphore_wait(barrier, len(everyone))

    def send(src, dst, slot, to):
        copy = pltpu.make_async_remote_copy(src, dst, send_sem.at[slot], recv_sem.at[slot], device_id=to, device_id_type=MESH)
        copy.start()
        return copy

    def rows(start, size):
        return pl.ds(pl.multiple_of(start, size), size)

    mine = core * half
    copy = send(a_ref.at[rows((1 - core) * half, half), :], got0, 0, sibling)
    copy.wait()
    acc[...] = a_ref[rows(mine, half), :] + got0[...]

    copies = [
        send(acc.at[rows(lax.rem(first + d, 4) * q1, q1), :], got1.at[d - 1], d, peer1(d)) for d in (1, 2, 3)
    ]
    for copy in copies:
        copy.wait()
    at1 = first * q1
    acc[rows(at1, q1), :] = (acc[rows(at1, q1), :] + got1[0]) + (got1[1] + got1[2])

    copies = [
        send(acc.at[rows(at1 + lax.rem(second + d, 4) * q2, q2), :], got2.at[d - 1], 3 + d, peer2(d)) for d in (1, 2, 3)
    ]
    for copy in copies:
        copy.wait()
    at2 = at1 + second * q2
    acc[rows(at2, q2), :] = (acc[rows(at2, q2), :] + got2[0]) + (got2[1] + got2[2])

    def columns(index):
        return pl.ds(pl.multiple_of(index * width, width), width)

    copies = [
        send(acc.at[rows(at2, q2), columns(lax.rem(z + d, 4))], got3.at[d - 1], 6 + d, peer3(d)) for d in (1, 2, 3)
    ]
    for copy in copies:
        copy.wait()
    out_ref[rows(mine + at2, q2), columns(z)] = (acc[rows(at2, q2), columns(z)] + got3[0]) + (got3[1] + got3[2])

    piece = out_ref.at[rows(mine + at2, q2), columns(z)]
    copies = [send(piece, piece, 9 + d, peer3(d)) for d in (1, 2, 3)]
    for copy in copies:
        copy.wait()
    piece = out_ref.at[rows(mine + at2, q2), :]
    copies = [send(piece, piece, 12 + d, peer2(d)) for d in (1, 2, 3)]
    for copy in copies:
        copy.wait()
    piece = out_ref.at[rows(mine + at1, q1), :]
    copies = [send(piece, piece, 15 + d, peer1(d)) for d in (1, 2, 3)]
    for copy in copies:
        copy.wait()
    piece = out_ref.at[rows(mine, half), :]
    copy = send(piece, piece, 19, sibling)
    copy.wait()


def sum_all(a):
    k, snaps = a.shape
    half = k // 2
    return pl.pallas_call(
        sum_kernel,
        out_shape=jax.ShapeDtypeStruct(a.shape, F32),
        in_specs=[VMEM],
        out_specs=VMEM,
        scratch_shapes=[
            pltpu.VMEM((half, snaps), F32),
            pltpu.VMEM((half, snaps), F32),
            pltpu.VMEM((3, half // 4, snaps), F32),
            pltpu.VMEM((3, half // 16, snaps), F32),
            pltpu.VMEM((3, half // 16, snaps // 4), F32),
            pltpu.SemaphoreType.DMA((20,)),
            pltpu.SemaphoreType.DMA((20,)),
        ],
        compiler_params=pltpu.CompilerParams(collective_id=1, has_side_effects=True, vmem_limit_bytes=32 << 20),
        name="sum_gram",
    )(a)


def factor_kernel(gram_ref, inverse_ref, work):
    b = 128
    work[:, :K] = gram_ref[...]
    r = lax.broadcasted_iota(jnp.int32, (K, K), 0)
    c = lax.broadcasted_iota(jnp.int32, (K, K), 1)
    work[:, K:] = jnp.where(r == c, 1.0, 0.0)
    sub = lax.broadcasted_iota(jnp.int32, (8, b), 0)
    lane = lax.broadcasted_iota(jnp.int32, (8, b), 1)
    groups = b // 8

    def block(k, carry):
        start = pl.multiple_of(k * b, b)
        s = [work[pl.ds(pl.multiple_of(start + 8 * g, 8), 8), pl.ds(start, b)] for g in range(groups)]
        e = [jnp.where(lane == sub + 8 * g, 1.0, 0.0) for g in range(groups)]
        t = [jnp.zeros((8, b), F32)] * groups
        for j in range(b):
            g0, r0 = j // 8, j % 8
            line = jnp.broadcast_to(s[g0][r0 : r0 + 1, :], (8, b))
            eline = jnp.broadcast_to(e[g0][r0 : r0 + 1, :], (8, b))
            pivot = jnp.broadcast_to(line[:, j : j + 1], (8, b))
            inv = 1.0 / pivot
            t[g0] = jnp.where(sub == r0, eline * lax.rsqrt(pivot), t[g0])
            line = line * inv
            eline = eline * inv
            for g in range(g0, groups):
                if g == g0 and r0 == 7:
                    continue
                m = jnp.broadcast_to(s[g][:, j : j + 1], (8, b))
                if g == g0:
                    m = jnp.where(sub > r0, m, 0.0)
                s[g] = s[g] - m * line
                e[g] = e[g] - m * eline
        top = jnp.concatenate(t, axis=0)
        upper = jnp.dot(top, work[pl.ds(start, b), :], precision=HIGH, preferred_element_type=F32)
        work[pl.ds(start, b), :] = upper
        inverse_ref[pl.ds(start, b), :] = upper[:, K:]
        left = work[pl.ds(start, b), :K]
        after = lax.broadcasted_iota(jnp.int32, (b, K), 1) >= start + b
        left = jnp.where(after, left, 0.0)
        work[...] = work[...] - lax.dot_general(left, upper, dims(0, 0), precision=HIGH, preferred_element_type=F32)
        return carry

    lax.fori_loop(0, K // b, block, 0)


def factor(gram):
    return pl.pallas_call(
        factor_kernel,
        grid=(1,),
        out_shape=jax.ShapeDtypeStruct((K, K), F32),
        in_specs=[pl.BlockSpec((K, K), lambda i: (0, 0))],
        out_specs=pl.BlockSpec((K, K), lambda i: (0, 0)),
        scratch_shapes=[pltpu.VMEM((K, 2 * K), F32)],
        compiler_params=pltpu.CompilerParams(vmem_limit_bytes=32 << 20),
        name="factor",
    )(gram)


def update_kernel(inverse_ref, left_ref, rows_ref, gram_ref, rest_ref, coef_ref, inv_hi, inv_lo, q_hi, q_lo):
    @pl.when(pl.program_id(0) == 0)
    def _():
        hi, lo = split2(inverse_ref[...])
        inv_hi[...], inv_lo[...] = hi, lo
        left_hi, left_lo = split2(left_ref[...])
        q = mm3(left_hi, left_lo, hi, lo, 1, 1)
        q_hi[...], q_lo[...] = split2(q)

    g_hi, g_lo = split2(gram_ref[...])
    coef = mm3(inv_hi[...], inv_lo[...], g_hi, g_lo)
    coef_ref[...] = coef
    c_hi, c_lo = split2(coef)
    rest = rows_ref[...] - mm3(q_hi[...], q_lo[...], c_hi, c_lo)
    rest_ref[...] = rest.reshape(rest_ref.shape)


def update(inverse, rows, gram, n_row):
    nodes, snaps = rows.shape
    n_blocks = snaps // NB
    per = nodes // n_row
    return pl.pallas_call(
        update_kernel,
        grid=(n_blocks,),
        out_shape=(
            jax.ShapeDtypeStruct((n_row, n_blocks, per, NB), F32),
            jax.ShapeDtypeStruct((K, snaps), F32),
        ),
        in_specs=[
            pl.BlockSpec((K, K), lambda i: (0, 0)),
            pl.BlockSpec((nodes, K), lambda i: (0, 0)),
            pl.BlockSpec((nodes, NB), lambda i: (0, i)),
            pl.BlockSpec((K, NB), lambda i: (0, i)),
        ],
        out_specs=(
            pl.BlockSpec((n_row, 1, per, NB), lambda i: (0, i, 0, 0)),
            pl.BlockSpec((K, NB), lambda i: (0, i)),
        ),
        scratch_shapes=[pltpu.VMEM((K, K), BF16)] * 2 + [pltpu.VMEM((nodes, K), BF16)] * 2,
        compiler_params=pltpu.CompilerParams(vmem_limit_bytes=32 << 20),
        name="update",
    )(inverse, rows, rows, gram)


def route_kernel(local_rows, per, target_ref, place_ref):
    row = lax.axis_index("row")
    target = target_ref[...]
    n, nodes = target.shape
    mask = jnp.where(target // local_rows == row, 1.0, 0.0)
    before = jnp.where(
        lax.broadcasted_iota(jnp.int32, (nodes, nodes), 0) < lax.broadcasted_iota(jnp.int32, (nodes, nodes), 1), 1.0, 0.0
    ).astype(BF16)
    rank = mm(mask.astype(BF16), before)
    rank = jnp.where(mask > 0.0, rank, -1.0)
    value = lax.rem(target, local_rows).astype(F32)
    lanes = lax.broadcasted_iota(jnp.int32, (n, per), 1)
    place = jnp.zeros((n, per), F32)
    for k in range(per):
        one = jnp.sum(jnp.where(rank == k, value, 0.0), axis=1, keepdims=True)
        place = jnp.where(lanes == k, one, place)
    place_ref[...] = place.astype(jnp.int32)


def route(target, n, local_rows, per):
    return pl.pallas_call(
        lambda *refs: route_kernel(local_rows, per, *refs),
        out_shape=jax.ShapeDtypeStruct((n, per), jnp.int32),
        in_specs=[VMEM],
        out_specs=VMEM,
        name="route",
    )(target.reshape(n, -1))


def place_kernel(place_ref, rows_ref, out_ref):
    n, per = place_ref.shape

    def body(s, carry):
        for k in range(per):
            out_ref[pl.ds(place_ref[s, k], 1), :] = rows_ref[pl.ds(s * per + k, 1), :]
        return carry

    lax.fori_loop(0, n, body, 0)


def place_rows(place, rows):
    return pl.pallas_call(
        place_kernel,
        out_shape=jax.ShapeDtypeStruct(rows.shape, F32),
        in_specs=[pl.BlockSpec(memory_space=pltpu.SMEM), VMEM],
        out_specs=VMEM,
        compiler_params=pltpu.CompilerParams(vmem_limit_bytes=32 << 20),
        name="place",
    )(place, rows)


def body(snapshots, district, target):
    n_row, n_col = lax.axis_size("row"), lax.axis_size("col")
    n = n_row * n_col
    nodes_dev, snaps = snapshots.shape
    local_rows = target.shape[0] // n_row
    per = nodes_dev // n_row
    me = lax.axis_index(("row", "col"))
    mine = lax.dynamic_slice_in_dim(target, me * nodes_dev, nodes_dev)
    weight = weights_of(district)
    rows, gram = prep(snapshots, weight, mine, n_row, local_rows)
    place = route(target, n, local_rows, per)
    gram = sum_all(gram)
    inverse = factor(gram)
    rest, coef = update(inverse, rows, gram, n_row)
    moved = lax.all_to_all(rest.reshape(n, per, NB), ("row", "col"), split_axis=0, concat_axis=0, tiled=True)
    remainder = place_rows(place, moved.reshape(n * per, NB))
    coefficients = lax.dynamic_slice_in_dim(coef, lax.axis_index("col") * NB, NB, axis=1)
    return coefficients, remainder


def solution(mesh):
    in_specs = (P(("row", "col"), None), P(("row", "col")), P())
    out_specs = (P(None, "col"), P("row", "col"))
    return jax.shard_map(body, mesh=mesh, in_specs=in_specs, out_specs=out_specs, check_vma=False)
```

```python
import jax
import jax.numpy as jnp
from jax import lax
from jax.experimental import pallas as pl
from jax.experimental.pallas import tpu as pltpu
from jax.sharding import PartitionSpec as P

MESH = pl.DeviceIdType.MESH
NB = 256
PANELS = 2
K = PANELS * NB
DIST_MEAN = 256
HIGH = lax.Precision.HIGHEST
F32 = jnp.float32
BF16 = jnp.bfloat16
VMEM = pl.BlockSpec(memory_space=pltpu.VMEM)


def split2(x):
    hi = x.astype(BF16)
    return hi, (x - hi.astype(F32)).astype(BF16)


def dims(a, b):
    return (((a,), (b,)), ((), ()))


def mm(x, y, a=1, b=0):
    return lax.dot_general(x, y, dims(a, b), preferred_element_type=F32)


def mm3(xh, xl, yh, yl, a=1, b=0):
    return mm(xh, yh, a, b) + (mm(xh, yl, a, b) + mm(xl, yh, a, b))


def counts_kernel(district_ref, weight_ref, own, got, send_sem, recv_sem):
    row, col = lax.axis_index("row"), lax.axis_index("col")
    n_row, n_col = lax.axis_size("row"), lax.axis_size("col")
    n = n_row * n_col
    me = row * n_col + col
    steps = (n - 2, n - 1, 1, 2)

    def peer(step):
        other = lax.rem(me + step, n)
        return other // n_col, lax.rem(other, n_col)

    barrier = pltpu.get_barrier_semaphore()
    for step in steps:
        pl.semaphore_signal(barrier, inc=1, device_id=peer(step), device_id_type=MESH)
    nodes = district_ref.shape[0]
    lanes = lax.broadcasted_iota(jnp.int32, (nodes, 256), 1)
    member = district_ref[...] == lanes
    hist = jnp.sum(jnp.where(member, 1.0, 0.0), axis=0, keepdims=True)
    own[...] = jnp.broadcast_to(hist, own.shape)
    pl.semaphore_wait(barrier, 4)
    copies = []
    for k, step in enumerate(steps):
        copy = pltpu.make_async_remote_copy(
            own, got.at[k], send_sem.at[k], recv_sem.at[k], device_id=peer(step), device_id_type=MESH
        )
        copy.start()
        copies.append(copy)
    for copy in copies:
        copy.wait()
    total = own[...]
    valid = (me + 2 < n, me + 1 < n, me >= 1, me >= 2)
    for k in range(4):
        total = total + got[k] * jnp.where(valid[k], 1.0, 0.0)
    scale = jnp.sqrt(DIST_MEAN / jnp.maximum(total, 1.0))[0:1, :]
    weight_ref[...] = jnp.sum(jnp.where(member, scale, 0.0), axis=1, keepdims=True)


def weights_of(district):
    nodes = district.shape[0]
    return pl.pallas_call(
        counts_kernel,
        out_shape=jax.ShapeDtypeStruct((nodes, 1), F32),
        in_specs=[VMEM],
        out_specs=VMEM,
        scratch_shapes=[
            pltpu.VMEM((8, 256), F32),
            pltpu.VMEM((4, 8, 256), F32),
            pltpu.SemaphoreType.DMA((4,)),
            pltpu.SemaphoreType.DMA((4,)),
        ],
        compiler_params=pltpu.CompilerParams(collective_id=0, has_side_effects=True),
        name="counts",
    )(district.reshape(nodes, 1))


def prep_kernel(local_rows, n_row, panel_ref, x_ref, weight_ref, target_ref, rows_ref, gram_ref, left_hi, left_lo, perm):
    nodes = x_ref.shape[0]
    per = nodes // n_row

    @pl.when(pl.program_id(0) == 0)
    def _():
        left = panel_ref[...] * weight_ref[...]
        hi, lo = split2(left)
        left_hi[...] = hi.T
        left_lo[...] = lo.T
        owner = target_ref[...] // local_rows
        groups = lax.broadcasted_iota(jnp.int32, (n_row, nodes), 0)
        mask = jnp.where(owner == groups, 1.0, 0.0)
        before = jnp.where(
            lax.broadcasted_iota(jnp.int32, (nodes, nodes), 0) < lax.broadcasted_iota(jnp.int32, (nodes, nodes), 1), 1.0, 0.0
        ).astype(BF16)
        rank = mm(mask.astype(BF16), before)
        base = groups.astype(F32) * per
        place = jnp.sum(mask * (rank + base), axis=0, keepdims=True).astype(jnp.int32)
        perm[...] = jnp.where(place == lax.broadcasted_iota(jnp.int32, (nodes, nodes), 0), 1.0, 0.0).astype(BF16)

    x = x_ref[...] * weight_ref[...]
    hi = x.astype(BF16)
    rest = x - hi.astype(F32)
    mid = rest.astype(BF16)
    low = (rest - mid.astype(F32)).astype(BF16)
    p = perm[...]
    rows_ref[...] = (mm(p, hi) + mm(p, mid)) + mm(p, low)
    gram_ref[...] = mm3(left_hi[...], left_lo[...], hi, mid)


def prep(snapshots, weight, mine, n_row, local_rows):
    nodes, snaps = snapshots.shape
    out = jax.ShapeDtypeStruct((nodes, snaps), F32), jax.ShapeDtypeStruct((K, snaps), F32)
    return pl.pallas_call(
        lambda *refs: prep_kernel(local_rows, n_row, *refs),
        grid=(snaps // NB,),
        out_shape=out,
        in_specs=[
            pl.BlockSpec((nodes, K), lambda i: (0, 0)),
            pl.BlockSpec((nodes, NB), lambda i: (0, i)),
            pl.BlockSpec((nodes, 1), lambda i: (0, 0)),
            pl.BlockSpec((1, nodes), lambda i: (0, 0)),
        ],
        out_specs=(pl.BlockSpec((nodes, NB), lambda i: (0, i)), pl.BlockSpec((K, NB), lambda i: (0, i))),
        scratch_shapes=[pltpu.VMEM((K, nodes), BF16), pltpu.VMEM((K, nodes), BF16), pltpu.VMEM((nodes, nodes), BF16)],
        compiler_params=pltpu.CompilerParams(vmem_limit_bytes=32 << 20),
        name="prep",
    )(snapshots, snapshots, weight, mine.reshape(1, nodes))


def sum_kernel(a_ref, out_ref, acc, got0, got1, got2, got3, send_sem, recv_sem):
    row, col = lax.axis_index("row"), lax.axis_index("col")
    y, x, z, core = row // 4, lax.rem(row, 4), col // 2, lax.rem(col, 2)
    half = a_ref.shape[0] // 2
    q1, q2 = half // 4, half // 16
    width = a_ref.shape[1] // 4
    first = (1 - core) * x + core * y
    second = (1 - core) * y + core * x

    def pair(p, q):
        return ((1 - core) * q + core * p) * 4 + (1 - core) * p + core * q

    def peer1(d):
        return pair(lax.rem(first + d, 4), second), col

    def peer2(d):
        return pair(first, lax.rem(second + d, 4)), col

    def peer3(d):
        return row, lax.rem(z + d, 4) * 2 + core

    sibling = (row, z * 2 + 1 - core)
    barrier = pltpu.get_barrier_semaphore()
    everyone = [sibling] + [peer(d) for peer in (peer1, peer2, peer3) for d in (1, 2, 3)]
    for one in everyone:
        pl.semaphore_signal(barrier, inc=1, device_id=one, device_id_type=MESH)
    pl.semaphore_wait(barrier, len(everyone))

    def send(src, dst, slot, to):
        copy = pltpu.make_async_remote_copy(src, dst, send_sem.at[slot], recv_sem.at[slot], device_id=to, device_id_type=MESH)
        copy.start()
        return copy

    def rows(start, size):
        return pl.ds(pl.multiple_of(start, size), size)

    mine = core * half
    copy = send(a_ref.at[rows((1 - core) * half, half), :], got0, 0, sibling)
    copy.wait()
    acc[...] = a_ref[rows(mine, half), :] + got0[...]

    copies = [
        send(acc.at[rows(lax.rem(first + d, 4) * q1, q1), :], got1.at[d - 1], d, peer1(d)) for d in (1, 2, 3)
    ]
    for copy in copies:
        copy.wait()
    at1 = first * q1
    acc[rows(at1, q1), :] = (acc[rows(at1, q1), :] + got1[0]) + (got1[1] + got1[2])

    copies = [
        send(acc.at[rows(at1 + lax.rem(second + d, 4) * q2, q2), :], got2.at[d - 1], 3 + d, peer2(d)) for d in (1, 2, 3)
    ]
    for copy in copies:
        copy.wait()
    at2 = at1 + second * q2
    acc[rows(at2, q2), :] = (acc[rows(at2, q2), :] + got2[0]) + (got2[1] + got2[2])

    def columns(index):
        return pl.ds(pl.multiple_of(index * width, width), width)

    copies = [
        send(acc.at[rows(at2, q2), columns(lax.rem(z + d, 4))], got3.at[d - 1], 6 + d, peer3(d)) for d in (1, 2, 3)
    ]
    for copy in copies:
        copy.wait()
    out_ref[rows(mine + at2, q2), columns(z)] = (acc[rows(at2, q2), columns(z)] + got3[0]) + (got3[1] + got3[2])

    piece = out_ref.at[rows(mine + at2, q2), columns(z)]
    copies = [send(piece, piece, 9 + d, peer3(d)) for d in (1, 2, 3)]
    for copy in copies:
        copy.wait()
    piece = out_ref.at[rows(mine + at2, q2), :]
    copies = [send(piece, piece, 12 + d, peer2(d)) for d in (1, 2, 3)]
    for copy in copies:
        copy.wait()
    piece = out_ref.at[rows(mine + at1, q1), :]
    copies = [send(piece, piece, 15 + d, peer1(d)) for d in (1, 2, 3)]
    for copy in copies:
        copy.wait()
    piece = out_ref.at[rows(mine, half), :]
    copy = send(piece, piece, 19, sibling)
    copy.wait()


def sum_all(a):
    k, snaps = a.shape
    half = k // 2
    return pl.pallas_call(
        sum_kernel,
        out_shape=jax.ShapeDtypeStruct(a.shape, F32),
        in_specs=[VMEM],
        out_specs=VMEM,
        scratch_shapes=[
            pltpu.VMEM((half, snaps), F32),
            pltpu.VMEM((half, snaps), F32),
            pltpu.VMEM((3, half // 4, snaps), F32),
            pltpu.VMEM((3, half // 16, snaps), F32),
            pltpu.VMEM((3, half // 16, snaps // 4), F32),
            pltpu.SemaphoreType.DMA((20,)),
            pltpu.SemaphoreType.DMA((20,)),
        ],
        compiler_params=pltpu.CompilerParams(collective_id=1, has_side_effects=True, vmem_limit_bytes=32 << 20),
        name="sum_gram",
    )(a)


def hdot(x, y, a=1, b=0):
    return lax.dot_general(x, y, dims(a, b), precision=HIGH, preferred_element_type=F32)


def eliminate(work, top, start):
    b=128; groups=b//8
    sub=lax.broadcasted_iota(jnp.int32,(8,b),0); lane=lax.broadcasted_iota(jnp.int32,(8,b),1)
    x=[work[pl.ds(pl.multiple_of(start+8*g,8),8), pl.ds(start,b)] for g in range(groups)]
    for g0 in range(groups):
        first=8*g0
        column=[[jnp.broadcast_to(x[g][:,first+c:first+c+1],(8,b)) for c in range(8)] for g in range(g0,groups)]
        inside=(lane>=first)&(lane<first+8)
        own=jnp.where(inside,jnp.where(lane-first==sub,1.0,0.0),x[g0])
        y=[jnp.broadcast_to(own[c:c+1,:],(8,b)) for c in range(8)]
        d=[[jnp.broadcast_to(column[0][k][c:c+1,:],(8,b)) for k in range(c+1)] for c in range(8)]
        inv=[]; low=[[None]*8 for _ in range(8)]
        for k in range(8):
            inv.append(1.0/d[k][k])
            for c in range(k+1,8):
                low[c][k]=d[c][k]*inv[k]
            for c in range(k+1,8):
                for m in range(k+1,c+1):
                    d[c][m]=d[c][m]-low[c][k]*d[m][k]
                y[c]=y[c]-low[c][k]*y[k]
        t=jnp.zeros((8,b),F32)
        for c in range(8):
            t=jnp.where(sub==c,y[c]*lax.rsqrt(d[c][c]),t)
        top[pl.ds(first,8),:]=jnp.where(lane<first+8,t,0.0)
        v=[None]*8
        for c in reversed(range(8)):
            a=y[c]*inv[c]
            for k in reversed(range(c+1,8)):
                a=a-low[k][c]*v[k]
            v[c]=a
        for g in range(g0+1,groups):
            m=column[g-g0]
            u=[m[c]*v[c] for c in range(8)]
            s=((u[0]+u[1])+(u[2]+u[3]))+((u[4]+u[5])+(u[6]+u[7]))
            x[g]=jnp.where(inside,0.0,x[g])-s
def factor_kernel(gram_ref, inverse_ref, work, top, upper):
    b=128
    work[...]=gram_ref[...]
    n=K//b
    def block(k,carry):
        start=pl.multiple_of(k*b,b)
        eliminate(work,top,start)
        cols=lax.broadcasted_iota(jnp.int32,(b,K),1)
        here=(cols>=start)&(cols<start+b)
        rows=lax.broadcasted_iota(jnp.int32,(b,K),0)
        line=jnp.where(here,jnp.where(cols-start==rows,1.0,0.0),work[pl.ds(start,b),:])
        up=hdot(top[...],line)
        upper[...]=up
        inverse_ref[pl.ds(start,b),:]=jnp.where(cols<start+b,up,0.0)
        def below(i,c):
            at=pl.multiple_of(i*b,b)
            left=upper[:,pl.ds(at,b)]
            work[pl.ds(at,b),:]=jnp.where(here,0.0,work[pl.ds(at,b),:])-hdot(left,upper[...],0,0)
            return c
        lax.fori_loop(k+1,n,below,0)
        return carry
    lax.fori_loop(0,n,block,0)

def factor(gram):
    return pl.pallas_call(
        factor_kernel,
        grid=(1,),
        out_shape=jax.ShapeDtypeStruct((K, K), F32),
        in_specs=[pl.BlockSpec((K, K), lambda i: (0, 0))],
        out_specs=pl.BlockSpec((K, K), lambda i: (0, 0)),
        scratch_shapes=[pltpu.VMEM((K, K), F32), pltpu.VMEM((128, 128), F32), pltpu.VMEM((128, K), F32)],
        compiler_params=pltpu.CompilerParams(vmem_limit_bytes=32 << 20),
        name="factor",
    )(gram)


def update_kernel(inverse_ref, left_ref, rows_ref, gram_ref, rest_ref, coef_ref, inv_hi, inv_lo, q_hi, q_lo):
    @pl.when(pl.program_id(0) == 0)
    def _():
        hi, lo = split2(inverse_ref[...])
        inv_hi[...], inv_lo[...] = hi, lo
        left_hi, left_lo = split2(left_ref[...])
        q = mm3(left_hi, left_lo, hi, lo, 1, 1)
        q_hi[...], q_lo[...] = split2(q)

    g_hi, g_lo = split2(gram_ref[...])
    coef = mm3(inv_hi[...], inv_lo[...], g_hi, g_lo)
    coef_ref[...] = coef
    c_hi, c_lo = split2(coef)
    rest = rows_ref[...] - mm3(q_hi[...], q_lo[...], c_hi, c_lo)
    rest_ref[...] = rest.reshape(rest_ref.shape)


def update(inverse, rows, gram, n_row):
    nodes, snaps = rows.shape
    n_blocks = snaps // NB
    per = nodes // n_row
    return pl.pallas_call(
        update_kernel,
        grid=(n_blocks,),
        out_shape=(
            jax.ShapeDtypeStruct((n_row, n_blocks, per, NB), F32),
            jax.ShapeDtypeStruct((K, snaps), F32),
        ),
        in_specs=[
            pl.BlockSpec((K, K), lambda i: (0, 0)),
            pl.BlockSpec((nodes, K), lambda i: (0, 0)),
            pl.BlockSpec((nodes, NB), lambda i: (0, i)),
            pl.BlockSpec((K, NB), lambda i: (0, i)),
        ],
        out_specs=(
            pl.BlockSpec((n_row, 1, per, NB), lambda i: (0, i, 0, 0)),
            pl.BlockSpec((K, NB), lambda i: (0, i)),
        ),
        scratch_shapes=[pltpu.VMEM((K, K), BF16)] * 2 + [pltpu.VMEM((nodes, K), BF16)] * 2,
        compiler_params=pltpu.CompilerParams(vmem_limit_bytes=32 << 20),
        name="update",
    )(inverse, rows, rows, gram)


def route_kernel(local_rows, per, target_ref, place_ref):
    row = lax.axis_index("row")
    target = target_ref[...]
    n, nodes = target.shape
    mask = jnp.where(target // local_rows == row, 1.0, 0.0)
    before = jnp.where(
        lax.broadcasted_iota(jnp.int32, (nodes, nodes), 0) < lax.broadcasted_iota(jnp.int32, (nodes, nodes), 1), 1.0, 0.0
    ).astype(BF16)
    rank = mm(mask.astype(BF16), before)
    rank = jnp.where(mask > 0.0, rank, -1.0)
    value = lax.rem(target, local_rows).astype(F32)
    lanes = lax.broadcasted_iota(jnp.int32, (n, per), 1)
    place = jnp.zeros((n, per), F32)
    for k in range(per):
        one = jnp.sum(jnp.where(rank == k, value, 0.0), axis=1, keepdims=True)
        place = jnp.where(lanes == k, one, place)
    place_ref[...] = place.astype(jnp.int32)


def route(target, n, local_rows, per):
    return pl.pallas_call(
        lambda *refs: route_kernel(local_rows, per, *refs),
        out_shape=jax.ShapeDtypeStruct((n, per), jnp.int32),
        in_specs=[VMEM],
        out_specs=VMEM,
        name="route",
    )(target.reshape(n, -1))


def place_kernel(place_ref, rows_ref, out_ref, inverse):
    n, per = place_ref.shape

    def invert(s, carry):
        for k in range(per):
            inverse[place_ref[s, k]] = s * per + k
        return carry

    lax.fori_loop(0, n, invert, 0)
    sub = lax.broadcasted_iota(jnp.int32, (8, NB), 0)

    def body(i, carry):
        for u in range(4):
            at = pl.multiple_of((i * 4 + u) * 8, 8)
            rows = jnp.broadcast_to(rows_ref[pl.ds(inverse[at], 1), :], (8, NB))
            for k in range(1, 8):
                rows = jnp.where(sub == k, jnp.broadcast_to(rows_ref[pl.ds(inverse[at + k], 1), :], (8, NB)), rows)
            out_ref[pl.ds(at, 8), :] = rows
        return carry

    lax.fori_loop(0, rows_ref.shape[0] // 32, body, 0)


def place_rows(place, rows):
    return pl.pallas_call(
        place_kernel,
        out_shape=jax.ShapeDtypeStruct(rows.shape, F32),
        in_specs=[pl.BlockSpec(memory_space=pltpu.SMEM), VMEM],
        out_specs=VMEM,
        scratch_shapes=[pltpu.SMEM((rows.shape[0],), jnp.int32)],
        compiler_params=pltpu.CompilerParams(vmem_limit_bytes=32 << 20),
        name="place",
    )(place, rows)


def body(snapshots, district, target):
    n_row, n_col = lax.axis_size("row"), lax.axis_size("col")
    n = n_row * n_col
    nodes_dev, snaps = snapshots.shape
    local_rows = target.shape[0] // n_row
    per = nodes_dev // n_row
    me = lax.axis_index(("row", "col"))
    mine = lax.dynamic_slice_in_dim(target, me * nodes_dev, nodes_dev)
    weight = weights_of(district)
    rows, gram = prep(snapshots, weight, mine, n_row, local_rows)
    place = route(target, n, local_rows, per)
    gram = sum_all(gram)
    inverse = factor(gram)
    rest, coef = update(inverse, rows, gram, n_row)
    moved = lax.all_to_all(rest.reshape(n, per, NB), ("row", "col"), split_axis=0, concat_axis=0, tiled=True)
    remainder = place_rows(place, moved.reshape(n * per, NB))
    coefficients = lax.dynamic_slice_in_dim(coef, lax.axis_index("col") * NB, NB, axis=1)
    return coefficients, remainder


def solution(mesh):
    in_specs = (P(("row", "col"), None), P(("row", "col")), P())
    out_specs = (P(None, "col"), P("row", "col"))
    return jax.shard_map(body, mesh=mesh, in_specs=in_specs, out_specs=out_specs, check_vma=False)
```

```python
import jax
import jax.numpy as jnp
from jax import lax
from jax.experimental import pallas as pl
from jax.experimental.pallas import tpu as pltpu
from jax.sharding import PartitionSpec as P

MESH = pl.DeviceIdType.MESH
NB = 256
PANELS = 2
K = PANELS * NB
DIST_MEAN = 256
HIGH = lax.Precision.HIGHEST
F32 = jnp.float32
BF16 = jnp.bfloat16
VMEM = pl.BlockSpec(memory_space=pltpu.VMEM)


def split2(x):
    hi = x.astype(BF16)
    return hi, (x - hi.astype(F32)).astype(BF16)


def dims(a, b):
    return (((a,), (b,)), ((), ()))


def mm(x, y, a=1, b=0):
    return lax.dot_general(x, y, dims(a, b), preferred_element_type=F32)


def mm3(xh, xl, yh, yl, a=1, b=0):
    return mm(xh, yh, a, b) + (mm(xh, yl, a, b) + mm(xl, yh, a, b))


def counts_kernel(district_ref, weight_ref, own, got, send_sem, recv_sem):
    row, col = lax.axis_index("row"), lax.axis_index("col")
    n_row, n_col = lax.axis_size("row"), lax.axis_size("col")
    n = n_row * n_col
    me = row * n_col + col
    steps = (n - 2, n - 1, 1, 2)

    def peer(step):
        other = lax.rem(me + step, n)
        return other // n_col, lax.rem(other, n_col)

    barrier = pltpu.get_barrier_semaphore()
    for step in steps:
        pl.semaphore_signal(barrier, inc=1, device_id=peer(step), device_id_type=MESH)
    nodes = district_ref.shape[0]
    lanes = lax.broadcasted_iota(jnp.int32, (nodes, 256), 1)
    member = district_ref[...] == lanes
    hist = jnp.sum(jnp.where(member, 1.0, 0.0), axis=0, keepdims=True)
    own[...] = jnp.broadcast_to(hist, own.shape)
    pl.semaphore_wait(barrier, 4)
    copies = []
    for k, step in enumerate(steps):
        copy = pltpu.make_async_remote_copy(
            own, got.at[k], send_sem.at[k], recv_sem.at[k], device_id=peer(step), device_id_type=MESH
        )
        copy.start()
        copies.append(copy)
    for copy in copies:
        copy.wait()
    total = own[...]
    valid = (me + 2 < n, me + 1 < n, me >= 1, me >= 2)
    for k in range(4):
        total = total + got[k] * jnp.where(valid[k], 1.0, 0.0)
    scale = jnp.sqrt(DIST_MEAN / jnp.maximum(total, 1.0))[0:1, :]
    weight_ref[...] = jnp.sum(jnp.where(member, scale, 0.0), axis=1, keepdims=True)


def weights_of(district):
    nodes = district.shape[0]
    return pl.pallas_call(
        counts_kernel,
        out_shape=jax.ShapeDtypeStruct((nodes, 1), F32),
        in_specs=[VMEM],
        out_specs=VMEM,
        scratch_shapes=[
            pltpu.VMEM((8, 256), F32),
            pltpu.VMEM((4, 8, 256), F32),
            pltpu.SemaphoreType.DMA((4,)),
            pltpu.SemaphoreType.DMA((4,)),
        ],
        compiler_params=pltpu.CompilerParams(collective_id=0, has_side_effects=True),
        name="counts",
    )(district.reshape(nodes, 1))


def prep_kernel(local_rows, n_row, panel_ref, x_ref, weight_ref, target_ref, rows_ref, gram_ref, left_hi, left_lo, perm):
    nodes = x_ref.shape[0]
    per = nodes // n_row

    @pl.when(pl.program_id(0) == 0)
    def _():
        left = panel_ref[...] * weight_ref[...]
        hi, lo = split2(left)
        left_hi[...] = hi.T
        left_lo[...] = lo.T
        owner = target_ref[...] // local_rows
        groups = lax.broadcasted_iota(jnp.int32, (n_row, nodes), 0)
        mask = jnp.where(owner == groups, 1.0, 0.0)
        before = jnp.where(
            lax.broadcasted_iota(jnp.int32, (nodes, nodes), 0) < lax.broadcasted_iota(jnp.int32, (nodes, nodes), 1), 1.0, 0.0
        ).astype(BF16)
        rank = mm(mask.astype(BF16), before)
        base = groups.astype(F32) * per
        place = jnp.sum(mask * (rank + base), axis=0, keepdims=True).astype(jnp.int32)
        perm[...] = jnp.where(place == lax.broadcasted_iota(jnp.int32, (nodes, nodes), 0), 1.0, 0.0).astype(BF16)

    x = x_ref[...] * weight_ref[...]
    hi = x.astype(BF16)
    rest = x - hi.astype(F32)
    mid = rest.astype(BF16)
    low = (rest - mid.astype(F32)).astype(BF16)
    p = perm[...]
    rows_ref[...] = (mm(p, hi) + mm(p, mid)) + mm(p, low)
    gram_ref[...] = mm3(left_hi[...], left_lo[...], hi, mid)


def prep(snapshots, weight, mine, n_row, local_rows):
    nodes, snaps = snapshots.shape
    out = jax.ShapeDtypeStruct((nodes, snaps), F32), jax.ShapeDtypeStruct((K, snaps), F32)
    return pl.pallas_call(
        lambda *refs: prep_kernel(local_rows, n_row, *refs),
        grid=(snaps // NB,),
        out_shape=out,
        in_specs=[
            pl.BlockSpec((nodes, K), lambda i: (0, 0)),
            pl.BlockSpec((nodes, NB), lambda i: (0, i)),
            pl.BlockSpec((nodes, 1), lambda i: (0, 0)),
            pl.BlockSpec((1, nodes), lambda i: (0, 0)),
        ],
        out_specs=(pl.BlockSpec((nodes, NB), lambda i: (0, i)), pl.BlockSpec((K, NB), lambda i: (0, i))),
        scratch_shapes=[pltpu.VMEM((K, nodes), BF16), pltpu.VMEM((K, nodes), BF16), pltpu.VMEM((nodes, nodes), BF16)],
        compiler_params=pltpu.CompilerParams(vmem_limit_bytes=32 << 20),
        name="prep",
    )(snapshots, snapshots, weight, mine.reshape(1, nodes))


def hdot(x, y, a=1, b=0):
    return lax.dot_general(x, y, dims(a, b), precision=HIGH, preferred_element_type=F32)


def eliminate(work, top, start, halfway):
    b=128; groups=b//8
    sub=lax.broadcasted_iota(jnp.int32,(8,b),0); lane=lax.broadcasted_iota(jnp.int32,(8,b),1)
    x=[work[pl.ds(pl.multiple_of(start+8*g,8),8), pl.ds(start,b)] for g in range(groups)]
    for g0 in range(groups):
        if g0 == groups // 2:
            halfway()
        first=8*g0
        column=[[jnp.broadcast_to(x[g][:,first+c:first+c+1],(8,b)) for c in range(8)] for g in range(g0,groups)]
        inside=(lane>=first)&(lane<first+8)
        own=jnp.where(inside,jnp.where(lane-first==sub,1.0,0.0),x[g0])
        y=[jnp.broadcast_to(own[c:c+1,:],(8,b)) for c in range(8)]
        d=[[jnp.broadcast_to(column[0][k][c:c+1,:],(8,b)) for k in range(c+1)] for c in range(8)]
        inv=[]; low=[[None]*8 for _ in range(8)]
        for k in range(8):
            inv.append(1.0/d[k][k])
            for c in range(k+1,8):
                low[c][k]=d[c][k]*inv[k]
            for c in range(k+1,8):
                for m in range(k+1,c+1):
                    d[c][m]=d[c][m]-low[c][k]*d[m][k]
                y[c]=y[c]-low[c][k]*y[k]
        t=jnp.zeros((8,b),F32)
        for c in range(8):
            t=jnp.where(sub==c,y[c]*lax.rsqrt(d[c][c]),t)
        top[pl.ds(first,8),:]=jnp.where(lane<first+8,t,0.0)
        v=[None]*8
        for c in reversed(range(8)):
            a=y[c]*inv[c]
            for k in reversed(range(c+1,8)):
                a=a-low[k][c]*v[k]
            v[c]=a
        for g in range(g0+1,groups):
            m=column[g-g0]
            u=[m[c]*v[c] for c in range(8)]
            s=((u[0]+u[1])+(u[2]+u[3]))+((u[4]+u[5])+(u[6]+u[7]))
            x[g]=jnp.where(inside,0.0,x[g])-s
def main_kernel(local_rows, per, gram_ref, rows_ref, target_ref, coef_ref, out_ref,
                full, got_core, acc, got_panel, got1, got2, got3, work, top, upper, inverse,
                inv_hi, inv_lo, q_hi, q_lo, stage, arrived0, arrived1, hot_row, hot_lo, hot_hi, index, index_smem,
                core_send, core_recv, panel_send, panel_recv, rest_send, rest_recv, row_send, row_recv, local_sem):
    row, col = lax.axis_index("row"), lax.axis_index("col")
    n_row, n_col = lax.axis_size("row"), lax.axis_size("col")
    me = row * n_col + col
    y, x, z, core = row // 4, lax.rem(row, 4), col // 2, lax.rem(col, 2)
    half = K // 2
    sibling = (row, z * 2 + 1 - core)
    mine = core * half

    def ds(start, size):
        return pl.ds(pl.multiple_of(start, size), size)

    def remote(src, dst, send, recv, to):
        return pltpu.make_async_remote_copy(src, dst, send, recv, device_id=to, device_id_type=MESH)

    def row_at(r):
        return lax.rem(y + r // 4, 4) * 4 + lax.rem(x + lax.rem(r, 4), 4)

    barrier = pltpu.get_barrier_semaphore()

    def greet(t, carry):
        to = (row_at(lax.rem(t, 16)), lax.rem(col + t // 16, n_col))
        pl.semaphore_signal(barrier, inc=1, device_id=to, device_id_type=MESH)
        return carry

    lax.fori_loop(1, n_row * n_col, greet, 0)
    pl.semaphore_wait(barrier, n_row * n_col - 1)

    def chunk(q):
        return pl.ds(q * K, K)

    def core_copy(q):
        return remote(gram_ref.at[ds((1 - core) * half, half), chunk(q)], got_core.at[q], core_send.at[q], core_recv.at[q], sibling)

    def core_back(q):
        piece = full.at[ds(mine, half), chunk(q)]
        return remote(piece, piece, core_send.at[4 + q], core_recv.at[4 + q], sibling)

    def take_core(q):
        core_copy(q).wait()
        acc[q] = gram_ref[ds(mine, half), chunk(q)] + got_core[q]

    def panel_peer(t):
        t = lax.rem(t * 29, 64)
        return row_at(lax.rem(t, 16)), lax.rem(z + t // 16, 4)

    def panel_out(t):
        r, c = panel_peer(t)
        src = acc.at[0, ds(r * 16, 16), ds(c * 128, 128)]
        return remote(src, got_panel.at[t], panel_send.at[0, t], panel_recv.at[0, t], (r, c * 2 + core))

    def panel_back(t):
        r, c = panel_peer(t)
        piece = full.at[ds(mine + row * 16, 16), ds(z * 128, 128)]
        return remote(piece, piece, panel_send.at[1, t], panel_recv.at[1, t], (r, c * 2 + core))

    def loop(lo, hi, act):
        def step(t, carry):
            act(t)
            return carry

        lax.fori_loop(lo, hi, step, 0)

    core_copy(0).start()
    for q in (1, 2, 3):
        core_copy(q).start()
    take_core(0)
    loop(1, 64, lambda t: panel_out(t).start())
    total = acc[0, ds(row * 16, 16), ds(z * 128, 128)]

    def add(t, total):
        panel_out(t).wait()
        return total + got_panel[t]

    total = lax.fori_loop(1, 64, add, total)
    full[ds(mine + row * 16, 16), ds(z * 128, 128)] = total
    loop(1, 64, lambda t: panel_back(t).start())

    def place_of(q):
        first = lax.rem(q + core, 3)
        out = []
        for k in range(3):
            axis = lax.rem(first + k, 3)
            ex, ey, ez = [jnp.where(axis == v, 1, 0) for v in range(3)]
            at = ex * x + ey * y + ez * z

            def peer(d, ex=ex, ey=ey, ez=ez):
                px, py, pz = lax.rem(x + d * ex, 4), lax.rem(y + d * ey, 4), lax.rem(z + d * ez, 4)
                return py * 4 + px, pz * 2 + core

            out.append((at, peer))
        return out

    where = {q: place_of(q) for q in (1, 2, 3)}
    DIST = (1, 2, 3)

    def rest_copies(q, stage_):
        (p1, peer1), (p2, peer2), (p3, peer3) = where[q]
        q1, q2 = half // 4, half // 16
        at1 = p1 * q1
        at2 = at1 + p2 * q2
        copies = []
        for d in DIST:
            slot = stage_ * 3 + d - 1
            sems = rest_send.at[q - 1, slot], rest_recv.at[q - 1, slot]
            if stage_ == 0:
                src, dst, to = acc.at[q, ds(lax.rem(p1 + d, 4) * q1, q1), :], got1.at[q - 1, d - 1], peer1(d)
            elif stage_ == 1:
                src, dst, to = acc.at[q, ds(at1 + lax.rem(p2 + d, 4) * q2, q2), :], got2.at[q - 1, d - 1], peer2(d)
            elif stage_ == 2:
                src = acc.at[q, ds(at2, q2), ds(lax.rem(p3 + d, 4) * 128, 128)]
                dst, to = got3.at[q - 1, d - 1], peer3(d)
            elif stage_ == 3:
                src = dst = full.at[ds(mine + at2, q2), pl.ds(pl.multiple_of(q * K + p3 * 128, 128), 128)]
                to = peer3(d)
            elif stage_ == 4:
                src = dst = full.at[ds(mine + at2, q2), chunk(q)]
                to = peer2(d)
            else:
                src = dst = full.at[ds(mine + at1, q1), chunk(q)]
                to = peer1(d)
            copies.append(remote(src, dst, *sems, to))
        return copies

    def start_rest(stage_):
        for q in (1, 2, 3):
            for copy in rest_copies(q, stage_):
                copy.start()

    def end_rest(stage_):
        for q in (1, 2, 3):
            for copy in rest_copies(q, stage_):
                copy.wait()

    def rest_step(k):
        if k == 0:
            for q in (1, 2, 3):
                take_core(q)
            start_rest(0)
        elif k <= 6:
            end_rest(k - 1)
            q1, q2 = half // 4, half // 16
            for q in (1, 2, 3):
                (p1, _), (p2, _), (p3, _) = where[q]
                at1, at2 = p1 * q1, p1 * q1 + p2 * q2
                if k == 1:
                    acc[q, ds(at1, q1), :] = (acc[q, ds(at1, q1), :] + got1[q - 1, 0]) + (got1[q - 1, 1] + got1[q - 1, 2])
                elif k == 2:
                    acc[q, ds(at2, q2), :] = (acc[q, ds(at2, q2), :] + got2[q - 1, 0]) + (got2[q - 1, 1] + got2[q - 1, 2])
                elif k == 3:
                    last = acc[q, ds(at2, q2), ds(p3 * 128, 128)]
                    full[ds(mine + at2, q2), pl.ds(pl.multiple_of(q * K + p3 * 128, 128), 128)] = (last + got3[q - 1, 0]) + (
                        got3[q - 1, 1] + got3[q - 1, 2]
                    )
            if k < 6:
                start_rest(k)
            else:
                for q in (1, 2, 3):
                    core_back(q).start()
        else:
            for q in (1, 2, 3):
                core_back(q).wait()

    loop(1, 64, lambda t: panel_back(t).wait())
    core_back(0).start()
    rest_step(0)
    core_back(0).wait()

    b = 128
    blocks = K // b
    work[...] = full[:, 0:K]
    cols = lax.broadcasted_iota(jnp.int32, (b, K), 1)
    lines = lax.broadcasted_iota(jnp.int32, (b, K), 0)

    def block(k, carry):
        start = pl.multiple_of(k * b, b)

        def at(k0, step):
            @pl.when(k == k0)
            def _():
                rest_step(step)

        def halfway():
            at(0, 1)
            at(1, 3)
            at(2, 5)
            at(3, 6)

        eliminate(work, top, start, halfway)
        here = (cols >= start) & (cols < start + b)
        line = jnp.where(here, jnp.where(cols - start == lines, 1.0, 0.0), work[pl.ds(start, b), :])
        up = hdot(top[...], line)
        upper[...] = up
        inverse[pl.ds(start, b), :] = jnp.where(cols < start + b, up, 0.0)

        def below(i, c):
            to = pl.multiple_of(i * b, b)
            left = upper[:, pl.ds(to, b)]
            work[pl.ds(to, b), :] = jnp.where(here, 0.0, work[pl.ds(to, b), :]) - hdot(left, upper[...], 0, 0)
            return c

        lax.fori_loop(k + 1, blocks, below, 0)
        at(0, 2)
        at(1, 4)
        return carry

    lax.fori_loop(0, blocks, block, 0)
    hi, lo = split2(inverse[...])
    inv_hi[...], inv_lo[...] = hi, lo
    left_hi, left_lo = split2(rows_ref[:, 0:K])
    q_hi[...], q_lo[...] = split2(mm3(left_hi, left_lo, hi, lo, 1, 1))
    rest_step(7)

    lanes = NB // 2
    arrived = (arrived0, arrived1)

    def message(j, t, h):
        r = row_at(lax.rem(t + 5 * j, 16))
        src = stage.at[j, h, ds(r * per, per), :]
        dst = arrived[h].at[ds(me * per, per), :]
        slot = j * 16 + t
        return remote(src, dst, row_send.at[h, slot], row_recv.at[h, slot], (r, lax.rem(col + j, n_col)))

    def own(h):
        return pltpu.make_async_copy(stage.at[0, h, ds(row * per, per), :], arrived[h].at[ds(me * per, per), :], local_sem.at[h])

    def form(j, carry):
        c = lax.rem(col + j, n_col)
        at = pl.ds(pl.multiple_of(c * NB, NB), NB)
        g_hi, g_lo = split2(full[:, at])
        coef = mm3(inv_hi[...], inv_lo[...], g_hi, g_lo)

        @pl.when(j == 0)
        def _():
            coef_ref[...] = coef

        c_hi, c_lo = split2(coef)
        rest = rows_ref[:, at] - mm3(q_hi[...], q_lo[...], c_hi, c_lo)
        stage[j, 0] = rest[:, :lanes]
        stage[j, 1] = rest[:, lanes:]

        @pl.when(j == 0)
        def _():
            own(0).start()
            own(1).start()

        def release(i, carry):
            message(i, j - i + 1, 0).start()
            return carry

        lax.fori_loop(0, j + 1, release, 0)
        return carry

    lax.fori_loop(0, n_col, form, 0)

    def late(t, carry):
        def one(j, carry):
            @pl.when(lax.rem(t, 16) + j > 8)
            def _():
                message(j, lax.rem(t, 16), 0).start()

            return carry

        lax.fori_loop(0, n_col, one, 0)
        return carry

    lax.fori_loop(1, 16, late, 0)
    loop(1, n_col, lambda j: message(j, 0, 0).start())

    def second(t, carry):
        loop(0, n_col, lambda j: message(j, t, 1).start())
        return carry

    lax.fori_loop(1, 16, second, 0)
    loop(1, n_col, lambda j: message(j, 0, 1).start())

    target = target_ref[...]
    n, nodes = target.shape
    mask = jnp.where(target // local_rows == row, 1.0, 0.0)
    before = jnp.where(
        lax.broadcasted_iota(jnp.int32, (nodes, nodes), 0) < lax.broadcasted_iota(jnp.int32, (nodes, nodes), 1), 1.0, 0.0
    ).astype(BF16)
    rank = jnp.where(mask > 0.0, mm(mask.astype(BF16), before), -1.0)
    value = lax.rem(target, local_rows).astype(F32)
    wide = lax.broadcasted_iota(jnp.int32, (n, 128), 1)
    source = lax.broadcasted_iota(jnp.int32, (n, 128), 0)
    for k in range(per):
        spot = jnp.sum(jnp.where(rank == float(k), value, 0.0), axis=1, keepdims=True).astype(jnp.int32)
        number = source * per + k
        low = wide == lax.rem(spot, 128)
        hot_row[pl.ds(k * n, n), :] = jnp.where(wide == spot // 128, 1.0, 0.0).astype(BF16)
        hot_lo[pl.ds(k * n, n), :] = jnp.where(low, lax.rem(number, 64).astype(F32), 0.0).astype(BF16)
        hot_hi[pl.ds(k * n, n), :] = jnp.where(low, (number // 64).astype(F32), 0.0).astype(BF16)
    hot = hot_row[...]
    found = mm(hot, hot_lo[...], 0, 0) + 64.0 * mm(hot, hot_hi[...], 0, 0)
    index[...] = jnp.clip(found[: local_rows // 128, :].astype(jnp.int32), 0, n * per - 1)
    to_smem = pltpu.make_async_copy(index, index_smem, local_sem.at[2])
    to_smem.start()
    to_smem.wait()

    sub = lax.broadcasted_iota(jnp.int32, (8, lanes), 0)
    for h in range(2):
        own(h).wait()

        def arrive(t, carry):
            loop(jnp.where(t == 0, 1, 0), n_col, lambda j: message(j, t, h).wait())
            return carry

        lax.fori_loop(0, 16, arrive, 0)

        def gather(i, carry):
            for u in range(16):
                rows = jnp.broadcast_to(arrived[h][pl.ds(index_smem[i, u * 8], 1), :], (8, lanes))
                for k in range(1, 8):
                    one = jnp.broadcast_to(arrived[h][pl.ds(index_smem[i, u * 8 + k], 1), :], (8, lanes))
                    rows = jnp.where(sub == k, one, rows)
                out_ref[pl.ds(pl.multiple_of(i * 128 + u * 8, 8), 8), pl.ds(h * lanes, lanes)] = rows
            return carry

        lax.fori_loop(0, local_rows // 128, gather, 0)


def finish(gram, rows, target, n_row, n_col):
    nodes, snaps = rows.shape
    n = n_row * n_col
    local_rows = target.shape[0] // n_row
    per = nodes // n_row
    half = K // 2
    dma = pltpu.SemaphoreType.DMA
    return pl.pallas_call(
        lambda *refs: main_kernel(local_rows, per, *refs),
        out_shape=(jax.ShapeDtypeStruct((K, NB), F32), jax.ShapeDtypeStruct((local_rows, NB), F32)),
        in_specs=[VMEM] * 3,
        out_specs=(VMEM, VMEM),
        scratch_shapes=[
            pltpu.VMEM((K, snaps), F32),
            pltpu.VMEM((4, half, K), F32),
            pltpu.VMEM((4, half, K), F32),
            pltpu.VMEM((64, 16, 128), F32),
            pltpu.VMEM((3, 3, half // 4, K), F32),
            pltpu.VMEM((3, 3, half // 16, K), F32),
            pltpu.VMEM((3, 3, half // 16, 128), F32),
            pltpu.VMEM((K, K), F32),
            pltpu.VMEM((128, 128), F32),
            pltpu.VMEM((128, K), F32),
            pltpu.VMEM((K, K), F32),
            pltpu.VMEM((K, K), BF16),
            pltpu.VMEM((K, K), BF16),
            pltpu.VMEM((nodes, K), BF16),
            pltpu.VMEM((nodes, K), BF16),
            pltpu.VMEM((n_col, 2, nodes, NB // 2), F32),
            pltpu.VMEM((n * per, NB // 2), F32),
            pltpu.VMEM((n * per, NB // 2), F32),
            pltpu.VMEM((n * per, 128), BF16),
            pltpu.VMEM((n * per, 128), BF16),
            pltpu.VMEM((n * per, 128), BF16),
            pltpu.VMEM((local_rows // 128, 128), jnp.int32),
            pltpu.SMEM((local_rows // 128, 128), jnp.int32),
            dma((8,)),
            dma((8,)),
            dma((2, 64)),
            dma((2, 64)),
            dma((3, 18)),
            dma((3, 18)),
            dma((2, 128)),
            dma((2, 128)),
            dma((3,)),
        ],
        compiler_params=pltpu.CompilerParams(collective_id=1, has_side_effects=True, vmem_limit_bytes=56 << 20),
        name="finish",
    )(gram, rows, target.reshape(n, nodes))


def body(snapshots, district, target):
    n_row, n_col = lax.axis_size("row"), lax.axis_size("col")
    nodes_dev, snaps = snapshots.shape
    local_rows = target.shape[0] // n_row
    me = lax.axis_index(("row", "col"))
    mine = lax.dynamic_slice_in_dim(target, me * nodes_dev, nodes_dev)
    weight = weights_of(district)
    rows, gram = prep(snapshots, weight, mine, n_row, local_rows)
    return finish(gram, rows, target, n_row, n_col)


def solution(mesh):
    in_specs = (P(("row", "col"), None), P(("row", "col")), P())
    out_specs = (P(None, "col"), P("row", "col"))
    return jax.shard_map(body, mesh=mesh, in_specs=in_specs, out_specs=out_specs, check_vma=False)
```

```python
import jax
import jax.numpy as jnp
from jax import lax
from jax.experimental import pallas as pl
from jax.experimental.pallas import tpu as pltpu
from jax.sharding import PartitionSpec as P

MESH = pl.DeviceIdType.MESH
NB = 256
PANELS = 2
K = PANELS * NB
DIST_MEAN = 256
HIGH = lax.Precision.HIGHEST
F32 = jnp.float32
BF16 = jnp.bfloat16
VMEM = pl.BlockSpec(memory_space=pltpu.VMEM)


def split2(x):
    hi = x.astype(BF16)
    return hi, (x - hi.astype(F32)).astype(BF16)


def dims(a, b):
    return (((a,), (b,)), ((), ()))


def mm(x, y, a=1, b=0):
    return lax.dot_general(x, y, dims(a, b), preferred_element_type=F32)


def mm3(xh, xl, yh, yl, a=1, b=0):
    return mm(xh, yh, a, b) + (mm(xh, yl, a, b) + mm(xl, yh, a, b))


def counts_kernel(district_ref, weight_ref, own, got, send_sem, recv_sem):
    row, col = lax.axis_index("row"), lax.axis_index("col")
    n_row, n_col = lax.axis_size("row"), lax.axis_size("col")
    n = n_row * n_col
    me = row * n_col + col
    steps = (n - 2, n - 1, 1, 2)

    def peer(step):
        other = lax.rem(me + step, n)
        return other // n_col, lax.rem(other, n_col)

    barrier = pltpu.get_barrier_semaphore()
    for step in steps:
        pl.semaphore_signal(barrier, inc=1, device_id=peer(step), device_id_type=MESH)
    nodes = district_ref.shape[0]
    lanes = lax.broadcasted_iota(jnp.int32, (nodes, 256), 1)
    member = district_ref[...] == lanes
    hist = jnp.sum(jnp.where(member, 1.0, 0.0), axis=0, keepdims=True)
    own[...] = jnp.broadcast_to(hist, own.shape)
    pl.semaphore_wait(barrier, 4)
    copies = []
    for k, step in enumerate(steps):
        copy = pltpu.make_async_remote_copy(
            own, got.at[k], send_sem.at[k], recv_sem.at[k], device_id=peer(step), device_id_type=MESH
        )
        copy.start()
        copies.append(copy)
    for copy in copies:
        copy.wait()
    total = own[...]
    valid = (me + 2 < n, me + 1 < n, me >= 1, me >= 2)
    for k in range(4):
        total = total + got[k] * jnp.where(valid[k], 1.0, 0.0)
    scale = jnp.sqrt(DIST_MEAN / jnp.maximum(total, 1.0))[0:1, :]
    weight_ref[...] = jnp.sum(jnp.where(member, scale, 0.0), axis=1, keepdims=True)


def weights_of(district):
    nodes = district.shape[0]
    return pl.pallas_call(
        counts_kernel,
        out_shape=jax.ShapeDtypeStruct((nodes, 1), F32),
        in_specs=[VMEM],
        out_specs=VMEM,
        scratch_shapes=[
            pltpu.VMEM((8, 256), F32),
            pltpu.VMEM((4, 8, 256), F32),
            pltpu.SemaphoreType.DMA((4,)),
            pltpu.SemaphoreType.DMA((4,)),
        ],
        compiler_params=pltpu.CompilerParams(collective_id=0, has_side_effects=True),
        name="counts",
    )(district.reshape(nodes, 1))


def hdot(x, y, a=1, b=0):
    return lax.dot_general(x, y, dims(a, b), precision=HIGH, preferred_element_type=F32)


def eliminate(work, top, start, halfway):
    b=128; groups=b//8
    sub=lax.broadcasted_iota(jnp.int32,(8,b),0); lane=lax.broadcasted_iota(jnp.int32,(8,b),1)
    x=[work[pl.ds(pl.multiple_of(start+8*g,8),8), pl.ds(start,b)] for g in range(groups)]
    for g0 in range(groups):
        if g0 == groups // 2:
            halfway()
        first=8*g0
        column=[[jnp.broadcast_to(x[g][:,first+c:first+c+1],(8,b)) for c in range(8)] for g in range(g0,groups)]
        inside=(lane>=first)&(lane<first+8)
        own=jnp.where(inside,jnp.where(lane-first==sub,1.0,0.0),x[g0])
        y=[jnp.broadcast_to(own[c:c+1,:],(8,b)) for c in range(8)]
        d=[[jnp.broadcast_to(column[0][k][c:c+1,:],(8,b)) for k in range(c+1)] for c in range(8)]
        inv=[]; low=[[None]*8 for _ in range(8)]
        for k in range(8):
            inv.append(1.0/d[k][k])
            for c in range(k+1,8):
                low[c][k]=d[c][k]*inv[k]
            for c in range(k+1,8):
                for m in range(k+1,c+1):
                    d[c][m]=d[c][m]-low[c][k]*d[m][k]
                y[c]=y[c]-low[c][k]*y[k]
        t=jnp.zeros((8,b),F32)
        for c in range(8):
            t=jnp.where(sub==c,y[c]*lax.rsqrt(d[c][c]),t)
        top[pl.ds(first,8),:]=jnp.where(lane<first+8,t,0.0)
        v=[None]*8
        for c in reversed(range(8)):
            a=y[c]*inv[c]
            for k in reversed(range(c+1,8)):
                a=a-low[k][c]*v[k]
            v[c]=a
        for g in range(g0+1,groups):
            m=column[g-g0]
            u=[m[c]*v[c] for c in range(8)]
            s=((u[0]+u[1])+(u[2]+u[3]))+((u[4]+u[5])+(u[6]+u[7]))
            x[g]=jnp.where(inside,0.0,x[g])-s
def main_kernel(local_rows, per, x_ref, weight_ref, mine_ref, target_ref, coef_ref, out_ref,
                rows_ref, gram_ref, left_hi, left_lo, perm, full, got_core, acc, got_panel, got1, got2, got3, work, top, upper, inverse,
                inv_hi, inv_lo, q_hi, q_lo, stage, arrived0, arrived1, hot_row, hot_lo, hot_hi, index, index_smem,
                core_send, core_recv, panel_send, panel_recv, rest_send, rest_recv, row_send, row_recv, local_sem):
    row, col = lax.axis_index("row"), lax.axis_index("col")
    n_row, n_col = lax.axis_size("row"), lax.axis_size("col")
    me = row * n_col + col
    y, x, z, core = row // 4, lax.rem(row, 4), col // 2, lax.rem(col, 2)
    half = K // 2
    sibling = (row, z * 2 + 1 - core)
    mine = core * half

    def ds(start, size):
        return pl.ds(pl.multiple_of(start, size), size)

    def remote(src, dst, send, recv, to):
        return pltpu.make_async_remote_copy(src, dst, send, recv, device_id=to, device_id_type=MESH)

    def row_at(r):
        return lax.rem(y + r // 4, 4) * 4 + lax.rem(x + lax.rem(r, 4), 4)

    barrier = pltpu.get_barrier_semaphore()

    def greet(t, carry):
        to = (row_at(lax.rem(t, 16)), lax.rem(col + t // 16, n_col))
        pl.semaphore_signal(barrier, inc=1, device_id=to, device_id_type=MESH)
        return carry

    lax.fori_loop(1, n_row * n_col, greet, 0)
    count = x_ref.shape[0]
    weight = jnp.broadcast_to(weight_ref[...], (count, NB))
    for k in range(PANELS):
        hi, lo = split2(x_ref[:, k * NB : (k + 1) * NB] * weight)
        left_hi[k * NB : (k + 1) * NB, :] = hi.T
        left_lo[k * NB : (k + 1) * NB, :] = lo.T
    groups = lax.broadcasted_iota(jnp.int32, (n_row, count), 0)
    belongs = jnp.where(mine_ref[...] // local_rows == groups, 1.0, 0.0)
    sooner = jnp.where(
        lax.broadcasted_iota(jnp.int32, (count, count), 0) < lax.broadcasted_iota(jnp.int32, (count, count), 1), 1.0, 0.0
    ).astype(BF16)
    spot = mm(belongs.astype(BF16), sooner) + (groups * per).astype(F32)
    spot = jnp.sum(belongs * spot, axis=0, keepdims=True).astype(jnp.int32)
    perm[...] = jnp.where(spot == lax.broadcasted_iota(jnp.int32, (count, count), 0), 1.0, 0.0).astype(BF16)

    def share(i, carry):
        at = pl.ds(pl.multiple_of(i * NB, NB), NB)
        v = x_ref[:, at] * weight
        hi = v.astype(BF16)
        rest = v - hi.astype(F32)
        mid = rest.astype(BF16)
        low = (rest - mid.astype(F32)).astype(BF16)
        p = perm[...]
        rows_ref[:, at] = (mm(p, hi) + mm(p, mid)) + mm(p, low)
        gram_ref[:, at] = mm3(left_hi[...], left_lo[...], hi, mid)
        return carry

    lax.fori_loop(0, x_ref.shape[1] // NB, share, 0)
    pl.semaphore_wait(barrier, n_row * n_col - 1)

    def chunk(q):
        return pl.ds(q * K, K)

    def core_copy(q):
        return remote(gram_ref.at[ds((1 - core) * half, half), chunk(q)], got_core.at[q], core_send.at[q], core_recv.at[q], sibling)

    def core_back(q):
        piece = full.at[ds(mine, half), chunk(q)]
        return remote(piece, piece, core_send.at[4 + q], core_recv.at[4 + q], sibling)

    def take_core(q):
        core_copy(q).wait()
        acc[q] = gram_ref[ds(mine, half), chunk(q)] + got_core[q]

    def panel_peer(t):
        t = lax.rem(t * 29, 64)
        return row_at(lax.rem(t, 16)), lax.rem(z + t // 16, 4)

    def panel_out(t):
        r, c = panel_peer(t)
        src = acc.at[0, ds(r * 16, 16), ds(c * 128, 128)]
        return remote(src, got_panel.at[t], panel_send.at[0, t], panel_recv.at[0, t], (r, c * 2 + core))

    def panel_back(t):
        r, c = panel_peer(t)
        piece = full.at[ds(mine + row * 16, 16), ds(z * 128, 128)]
        return remote(piece, piece, panel_send.at[1, t], panel_recv.at[1, t], (r, c * 2 + core))

    def loop(lo, hi, act):
        def step(t, carry):
            act(t)
            return carry

        lax.fori_loop(lo, hi, step, 0)

    core_copy(0).start()
    for q in (1, 2, 3):
        core_copy(q).start()
    take_core(0)
    loop(1, 64, lambda t: panel_out(t).start())
    total = acc[0, ds(row * 16, 16), ds(z * 128, 128)]

    def add(t, total):
        panel_out(t).wait()
        return total + got_panel[t]

    total = lax.fori_loop(1, 64, add, total)
    full[ds(mine + row * 16, 16), ds(z * 128, 128)] = total
    loop(1, 64, lambda t: panel_back(t).start())

    def place_of(q):
        first = lax.rem(q + core, 3)
        out = []
        for k in range(3):
            axis = lax.rem(first + k, 3)
            ex, ey, ez = [jnp.where(axis == v, 1, 0) for v in range(3)]
            at = ex * x + ey * y + ez * z

            def peer(d, ex=ex, ey=ey, ez=ez):
                px, py, pz = lax.rem(x + d * ex, 4), lax.rem(y + d * ey, 4), lax.rem(z + d * ez, 4)
                return py * 4 + px, pz * 2 + core

            out.append((at, peer))
        return out

    where = {q: place_of(q) for q in (1, 2, 3)}
    DIST = (1, 2, 3)

    def rest_copies(q, stage_):
        (p1, peer1), (p2, peer2), (p3, peer3) = where[q]
        q1, q2 = half // 4, half // 16
        at1 = p1 * q1
        at2 = at1 + p2 * q2
        copies = []
        for d in DIST:
            slot = stage_ * 3 + d - 1
            sems = rest_send.at[q - 1, slot], rest_recv.at[q - 1, slot]
            if stage_ == 0:
                src, dst, to = acc.at[q, ds(lax.rem(p1 + d, 4) * q1, q1), :], got1.at[q - 1, d - 1], peer1(d)
            elif stage_ == 1:
                src, dst, to = acc.at[q, ds(at1 + lax.rem(p2 + d, 4) * q2, q2), :], got2.at[q - 1, d - 1], peer2(d)
            elif stage_ == 2:
                src = acc.at[q, ds(at2, q2), ds(lax.rem(p3 + d, 4) * 128, 128)]
                dst, to = got3.at[q - 1, d - 1], peer3(d)
            elif stage_ == 3:
                src = dst = full.at[ds(mine + at2, q2), pl.ds(pl.multiple_of(q * K + p3 * 128, 128), 128)]
                to = peer3(d)
            elif stage_ == 4:
                src = dst = full.at[ds(mine + at2, q2), chunk(q)]
                to = peer2(d)
            else:
                src = dst = full.at[ds(mine + at1, q1), chunk(q)]
                to = peer1(d)
            copies.append(remote(src, dst, *sems, to))
        return copies

    def start_rest(stage_):
        for q in (1, 2, 3):
            for copy in rest_copies(q, stage_):
                copy.start()

    def end_rest(stage_):
        for q in (1, 2, 3):
            for copy in rest_copies(q, stage_):
                copy.wait()

    def rest_step(k):
        if k == 0:
            for q in (1, 2, 3):
                take_core(q)
            start_rest(0)
        elif k <= 6:
            end_rest(k - 1)
            q1, q2 = half // 4, half // 16
            for q in (1, 2, 3):
                (p1, _), (p2, _), (p3, _) = where[q]
                at1, at2 = p1 * q1, p1 * q1 + p2 * q2
                if k == 1:
                    acc[q, ds(at1, q1), :] = (acc[q, ds(at1, q1), :] + got1[q - 1, 0]) + (got1[q - 1, 1] + got1[q - 1, 2])
                elif k == 2:
                    acc[q, ds(at2, q2), :] = (acc[q, ds(at2, q2), :] + got2[q - 1, 0]) + (got2[q - 1, 1] + got2[q - 1, 2])
                elif k == 3:
                    last = acc[q, ds(at2, q2), ds(p3 * 128, 128)]
                    full[ds(mine + at2, q2), pl.ds(pl.multiple_of(q * K + p3 * 128, 128), 128)] = (last + got3[q - 1, 0]) + (
                        got3[q - 1, 1] + got3[q - 1, 2]
                    )
            if k < 6:
                start_rest(k)
            else:
                for q in (1, 2, 3):
                    core_back(q).start()
        else:
            for q in (1, 2, 3):
                core_back(q).wait()

    loop(1, 64, lambda t: panel_back(t).wait())
    core_back(0).start()
    rest_step(0)
    core_back(0).wait()

    b = 128
    blocks = K // b
    work[...] = full[:, 0:K]
    cols = lax.broadcasted_iota(jnp.int32, (b, K), 1)
    lines = lax.broadcasted_iota(jnp.int32, (b, K), 0)

    def block(k, carry):
        start = pl.multiple_of(k * b, b)

        def at(k0, step):
            @pl.when(k == k0)
            def _():
                rest_step(step)

        def halfway():
            at(0, 1)
            at(1, 3)
            at(2, 5)
            at(3, 6)

        eliminate(work, top, start, halfway)
        here = (cols >= start) & (cols < start + b)
        line = jnp.where(here, jnp.where(cols - start == lines, 1.0, 0.0), work[pl.ds(start, b), :])
        up = hdot(top[...], line)
        upper[...] = up
        inverse[pl.ds(start, b), :] = jnp.where(cols < start + b, up, 0.0)

        def below(i, c):
            to = pl.multiple_of(i * b, b)
            left = upper[:, pl.ds(to, b)]
            work[pl.ds(to, b), :] = jnp.where(here, 0.0, work[pl.ds(to, b), :]) - hdot(left, upper[...], 0, 0)
            return c

        lax.fori_loop(k + 1, blocks, below, 0)
        at(0, 2)
        at(1, 4)
        return carry

    lax.fori_loop(0, blocks, block, 0)
    hi, lo = split2(inverse[...])
    inv_hi[...], inv_lo[...] = hi, lo
    left_hi, left_lo = split2(rows_ref[:, 0:K])
    q_hi[...], q_lo[...] = split2(mm3(left_hi, left_lo, hi, lo, 1, 1))
    rest_step(7)

    lanes = NB // 2
    arrived = (arrived0, arrived1)

    def message(j, t, h):
        r = row_at(lax.rem(t + 5 * j, 16))
        src = stage.at[j, h, ds(r * per, per), :]
        dst = arrived[h].at[ds(me * per, per), :]
        slot = j * 16 + t
        return remote(src, dst, row_send.at[h, slot], row_recv.at[h, slot], (r, lax.rem(col + j, n_col)))

    def own(h):
        return pltpu.make_async_copy(stage.at[0, h, ds(row * per, per), :], arrived[h].at[ds(me * per, per), :], local_sem.at[h])

    def form(j, carry):
        c = lax.rem(col + j, n_col)
        at = pl.ds(pl.multiple_of(c * NB, NB), NB)
        g_hi, g_lo = split2(full[:, at])
        coef = mm3(inv_hi[...], inv_lo[...], g_hi, g_lo)

        @pl.when(j == 0)
        def _():
            coef_ref[...] = coef

        c_hi, c_lo = split2(coef)
        rest = rows_ref[:, at] - mm3(q_hi[...], q_lo[...], c_hi, c_lo)
        stage[j, 0] = rest[:, :lanes]
        stage[j, 1] = rest[:, lanes:]

        @pl.when(j == 0)
        def _():
            own(0).start()
            own(1).start()

        def release(i, carry):
            message(i, j - i + 1, 0).start()
            return carry

        lax.fori_loop(0, j + 1, release, 0)
        return carry

    lax.fori_loop(0, n_col, form, 0)

    def late(t, carry):
        def one(j, carry):
            @pl.when(lax.rem(t, 16) + j > 8)
            def _():
                message(j, lax.rem(t, 16), 0).start()

            return carry

        lax.fori_loop(0, n_col, one, 0)
        return carry

    lax.fori_loop(1, 16, late, 0)
    loop(1, n_col, lambda j: message(j, 0, 0).start())

    def second(t, carry):
        loop(0, n_col, lambda j: message(j, t, 1).start())
        return carry

    lax.fori_loop(1, 16, second, 0)
    loop(1, n_col, lambda j: message(j, 0, 1).start())

    target = target_ref[...]
    n, nodes = target.shape
    mask = jnp.where(target // local_rows == row, 1.0, 0.0)
    before = jnp.where(
        lax.broadcasted_iota(jnp.int32, (nodes, nodes), 0) < lax.broadcasted_iota(jnp.int32, (nodes, nodes), 1), 1.0, 0.0
    ).astype(BF16)
    rank = jnp.where(mask > 0.0, mm(mask.astype(BF16), before), -1.0)
    value = lax.rem(target, local_rows).astype(F32)
    wide = lax.broadcasted_iota(jnp.int32, (n, 128), 1)
    source = lax.broadcasted_iota(jnp.int32, (n, 128), 0)
    for k in range(per):
        spot = jnp.sum(jnp.where(rank == float(k), value, 0.0), axis=1, keepdims=True).astype(jnp.int32)
        number = source * per + k
        low = wide == lax.rem(spot, 128)
        hot_row[pl.ds(k * n, n), :] = jnp.where(wide == spot // 128, 1.0, 0.0).astype(BF16)
        hot_lo[pl.ds(k * n, n), :] = jnp.where(low, lax.rem(number, 64).astype(F32), 0.0).astype(BF16)
        hot_hi[pl.ds(k * n, n), :] = jnp.where(low, (number // 64).astype(F32), 0.0).astype(BF16)
    hot = hot_row[...]
    found = mm(hot, hot_lo[...], 0, 0) + 64.0 * mm(hot, hot_hi[...], 0, 0)
    index[...] = jnp.clip(found[: local_rows // 128, :].astype(jnp.int32), 0, n * per - 1)
    to_smem = pltpu.make_async_copy(index, index_smem, local_sem.at[2])
    to_smem.start()
    to_smem.wait()

    sub = lax.broadcasted_iota(jnp.int32, (8, lanes), 0)
    for h in range(2):
        own(h).wait()

        def arrive(t, carry):
            loop(jnp.where(t == 0, 1, 0), n_col, lambda j: message(j, t, h).wait())
            return carry

        lax.fori_loop(0, 16, arrive, 0)

        def gather(i, carry):
            for u in range(16):
                rows = jnp.broadcast_to(arrived[h][pl.ds(index_smem[i, u * 8], 1), :], (8, lanes))
                for k in range(1, 8):
                    one = jnp.broadcast_to(arrived[h][pl.ds(index_smem[i, u * 8 + k], 1), :], (8, lanes))
                    rows = jnp.where(sub == k, one, rows)
                out_ref[pl.ds(pl.multiple_of(i * 128 + u * 8, 8), 8), pl.ds(h * lanes, lanes)] = rows
            return carry

        lax.fori_loop(0, local_rows // 128, gather, 0)


def finish(snapshots, weight, mine, target, n_row, n_col):
    nodes, snaps = snapshots.shape
    n = n_row * n_col
    local_rows = target.shape[0] // n_row
    per = nodes // n_row
    half = K // 2
    dma = pltpu.SemaphoreType.DMA
    return pl.pallas_call(
        lambda *refs: main_kernel(local_rows, per, *refs),
        out_shape=(jax.ShapeDtypeStruct((K, NB), F32), jax.ShapeDtypeStruct((local_rows, NB), F32)),
        in_specs=[VMEM] * 4,
        out_specs=(VMEM, VMEM),
        scratch_shapes=[
            pltpu.VMEM((nodes, snaps), F32),
            pltpu.VMEM((K, snaps), F32),
            pltpu.VMEM((K, nodes), BF16),
            pltpu.VMEM((K, nodes), BF16),
            pltpu.VMEM((nodes, nodes), BF16),
            pltpu.VMEM((K, snaps), F32),
            pltpu.VMEM((4, half, K), F32),
            pltpu.VMEM((4, half, K), F32),
            pltpu.VMEM((64, 16, 128), F32),
            pltpu.VMEM((3, 3, half // 4, K), F32),
            pltpu.VMEM((3, 3, half // 16, K), F32),
            pltpu.VMEM((3, 3, half // 16, 128), F32),
            pltpu.VMEM((K, K), F32),
            pltpu.VMEM((128, 128), F32),
            pltpu.VMEM((128, K), F32),
            pltpu.VMEM((K, K), F32),
            pltpu.VMEM((K, K), BF16),
            pltpu.VMEM((K, K), BF16),
            pltpu.VMEM((nodes, K), BF16),
            pltpu.VMEM((nodes, K), BF16),
            pltpu.VMEM((n_col, 2, nodes, NB // 2), F32),
            pltpu.VMEM((n * per, NB // 2), F32),
            pltpu.VMEM((n * per, NB // 2), F32),
            pltpu.VMEM((n * per, 128), BF16),
            pltpu.VMEM((n * per, 128), BF16),
            pltpu.VMEM((n * per, 128), BF16),
            pltpu.VMEM((local_rows // 128, 128), jnp.int32),
            pltpu.SMEM((local_rows // 128, 128), jnp.int32),
            dma((8,)),
            dma((8,)),
            dma((2, 64)),
            dma((2, 64)),
            dma((3, 18)),
            dma((3, 18)),
            dma((2, 128)),
            dma((2, 128)),
            dma((3,)),
        ],
        compiler_params=pltpu.CompilerParams(collective_id=1, has_side_effects=True, vmem_limit_bytes=46 << 20),
        name="finish",
    )(snapshots, weight, mine.reshape(1, nodes), target.reshape(n, nodes))


def body(snapshots, district, target):
    n_row, n_col = lax.axis_size("row"), lax.axis_size("col")
    nodes_dev, snaps = snapshots.shape
    me = lax.axis_index(("row", "col"))
    mine = lax.dynamic_slice_in_dim(target, me * nodes_dev, nodes_dev)
    weight = weights_of(district)
    return finish(snapshots, weight, mine, target, n_row, n_col)


def solution(mesh):
    in_specs = (P(("row", "col"), None), P(("row", "col")), P())
    out_specs = (P(None, "col"), P("row", "col"))
    return jax.shard_map(body, mesh=mesh, in_specs=in_specs, out_specs=out_specs, check_vma=False)
```

```python
import jax
import jax.numpy as jnp
from jax import lax
from jax.experimental import pallas as pl
from jax.experimental.pallas import tpu as pltpu
from jax.sharding import PartitionSpec as P

MESH = pl.DeviceIdType.MESH
NB = 256
PANELS = 2
K = PANELS * NB
DIST_MEAN = 256
HIGH = lax.Precision.HIGHEST
F32 = jnp.float32
BF16 = jnp.bfloat16
VMEM = pl.BlockSpec(memory_space=pltpu.VMEM)


def split2(x):
    hi = x.astype(BF16)
    return hi, (x - hi.astype(F32)).astype(BF16)


def dims(a, b):
    return (((a,), (b,)), ((), ()))


def mm(x, y, a=1, b=0):
    return lax.dot_general(x, y, dims(a, b), preferred_element_type=F32)


def mm3(xh, xl, yh, yl, a=1, b=0):
    return mm(xh, yh, a, b) + (mm(xh, yl, a, b) + mm(xl, yh, a, b))


def counts_kernel(district_ref, weight_ref, own, got, send_sem, recv_sem):
    row, col = lax.axis_index("row"), lax.axis_index("col")
    n_row, n_col = lax.axis_size("row"), lax.axis_size("col")
    n = n_row * n_col
    me = row * n_col + col
    steps = (n - 2, n - 1, 1, 2)

    def peer(step):
        other = lax.rem(me + step, n)
        return other // n_col, lax.rem(other, n_col)

    barrier = pltpu.get_barrier_semaphore()
    for step in steps:
        pl.semaphore_signal(barrier, inc=1, device_id=peer(step), device_id_type=MESH)
    nodes = district_ref.shape[0]
    lanes = lax.broadcasted_iota(jnp.int32, (nodes, 256), 1)
    member = district_ref[...] == lanes
    hist = jnp.sum(jnp.where(member, 1.0, 0.0), axis=0, keepdims=True)
    own[...] = jnp.broadcast_to(hist, own.shape)
    pl.semaphore_wait(barrier, 4)
    copies = []
    for k, step in enumerate(steps):
        copy = pltpu.make_async_remote_copy(
            own, got.at[k], send_sem.at[k], recv_sem.at[k], device_id=peer(step), device_id_type=MESH
        )
        copy.start()
        copies.append(copy)
    for copy in copies:
        copy.wait()
    total = own[...]
    valid = (me + 2 < n, me + 1 < n, me >= 1, me >= 2)
    for k in range(4):
        total = total + got[k] * jnp.where(valid[k], 1.0, 0.0)
    scale = jnp.sqrt(DIST_MEAN / jnp.maximum(total, 1.0))[0:1, :]
    weight_ref[...] = jnp.sum(jnp.where(member, scale, 0.0), axis=1, keepdims=True)


def weights_of(district):
    nodes = district.shape[0]
    return pl.pallas_call(
        counts_kernel,
        out_shape=jax.ShapeDtypeStruct((nodes, 1), F32),
        in_specs=[VMEM],
        out_specs=VMEM,
        scratch_shapes=[
            pltpu.VMEM((8, 256), F32),
            pltpu.VMEM((4, 8, 256), F32),
            pltpu.SemaphoreType.DMA((4,)),
            pltpu.SemaphoreType.DMA((4,)),
        ],
        compiler_params=pltpu.CompilerParams(collective_id=0, has_side_effects=True),
        name="counts",
    )(district.reshape(nodes, 1))


def hdot(x, y, a=1, b=0):
    return lax.dot_general(x, y, dims(a, b), precision=HIGH, preferred_element_type=F32)


def eliminate(work, top, start, halfway):
    b=128; groups=b//8
    sub=lax.broadcasted_iota(jnp.int32,(8,b),0); lane=lax.broadcasted_iota(jnp.int32,(8,b),1)
    x=[work[pl.ds(pl.multiple_of(start+8*g,8),8), pl.ds(start,b)] for g in range(groups)]
    for g0 in range(groups):
        if g0 == groups // 2:
            halfway()
        first=8*g0
        column=[[jnp.broadcast_to(x[g][:,first+c:first+c+1],(8,b)) for c in range(8)] for g in range(g0,groups)]
        inside=(lane>=first)&(lane<first+8)
        own=jnp.where(inside,jnp.where(lane-first==sub,1.0,0.0),x[g0])
        y=[jnp.broadcast_to(own[c:c+1,:],(8,b)) for c in range(8)]
        d=[[jnp.broadcast_to(column[0][k][c:c+1,:],(8,b)) for k in range(c+1)] for c in range(8)]
        inv=[]; low=[[None]*8 for _ in range(8)]
        for k in range(8):
            inv.append(1.0/d[k][k])
            for c in range(k+1,8):
                low[c][k]=d[c][k]*inv[k]
            for c in range(k+1,8):
                for m in range(k+1,c+1):
                    d[c][m]=d[c][m]-low[c][k]*d[m][k]
                y[c]=y[c]-low[c][k]*y[k]
        t=jnp.zeros((8,b),F32)
        for c in range(8):
            t=jnp.where(sub==c,y[c]*lax.rsqrt(d[c][c]),t)
        top[pl.ds(first,8),:]=jnp.where(lane<first+8,t,0.0)
        v=[None]*8
        for c in reversed(range(8)):
            a=y[c]*inv[c]
            for k in reversed(range(c+1,8)):
                a=a-low[k][c]*v[k]
            v[c]=a
        for g in range(g0+1,groups):
            m=column[g-g0]
            u=[m[c]*v[c] for c in range(8)]
            s=((u[0]+u[1])+(u[2]+u[3]))+((u[4]+u[5])+(u[6]+u[7]))
            x[g]=jnp.where(inside,0.0,x[g])-s
def main_kernel(local_rows, per, x_ref, weight_ref, mine_ref, target_ref, coef_ref, out_ref,
                rows_ref, gram_ref, left_hi, left_lo, perm, full, got_core, acc, got_panel, got1, got2, got3, work, top, upper, inverse,
                inv_hi, inv_lo, q_hi, q_lo, stage, arrived0, arrived1, hot_row, hot_lo, hot_hi, index, index_smem,
                core_send, core_recv, panel_send, panel_recv, rest_send, rest_recv, row_send, row_recv, local_sem):
    row, col = lax.axis_index("row"), lax.axis_index("col")
    n_row, n_col = lax.axis_size("row"), lax.axis_size("col")
    me = row * n_col + col
    y, x, z, core = row // 4, lax.rem(row, 4), col // 2, lax.rem(col, 2)
    half = K // 2
    sibling = (row, z * 2 + 1 - core)
    mine = core * half

    def ds(start, size):
        return pl.ds(pl.multiple_of(start, size), size)

    def remote(src, dst, send, recv, to):
        return pltpu.make_async_remote_copy(src, dst, send, recv, device_id=to, device_id_type=MESH)

    def row_at(r):
        return lax.rem(y + r // 4, 4) * 4 + lax.rem(x + lax.rem(r, 4), 4)

    barrier = pltpu.get_barrier_semaphore()

    def greet(t, carry):
        to = (row_at(lax.rem(t, 16)), lax.rem(col + t // 16, n_col))
        pl.semaphore_signal(barrier, inc=1, device_id=to, device_id_type=MESH)
        return carry

    lax.fori_loop(1, n_row * n_col, greet, 0)
    count = x_ref.shape[0]
    weight = jnp.broadcast_to(weight_ref[...], (count, NB))
    for k in range(PANELS):
        hi, lo = split2(x_ref[:, k * NB : (k + 1) * NB] * weight)
        left_hi[k * NB : (k + 1) * NB, :] = hi.T
        left_lo[k * NB : (k + 1) * NB, :] = lo.T
    groups = lax.broadcasted_iota(jnp.int32, (n_row, count), 0)
    belongs = jnp.where(mine_ref[...] // local_rows == groups, 1.0, 0.0)
    sooner = jnp.where(
        lax.broadcasted_iota(jnp.int32, (count, count), 0) < lax.broadcasted_iota(jnp.int32, (count, count), 1), 1.0, 0.0
    ).astype(BF16)
    spot = mm(belongs.astype(BF16), sooner) + (groups * per).astype(F32)
    spot = jnp.sum(belongs * spot, axis=0, keepdims=True).astype(jnp.int32)
    perm[...] = jnp.where(spot == lax.broadcasted_iota(jnp.int32, (count, count), 0), 1.0, 0.0).astype(BF16)

    def share(i, carry):
        at = pl.ds(pl.multiple_of(i * NB, NB), NB)
        v = x_ref[:, at] * weight
        hi = v.astype(BF16)
        rest = v - hi.astype(F32)
        mid = rest.astype(BF16)
        low = (rest - mid.astype(F32)).astype(BF16)
        p = perm[...]
        rows_ref[:, at] = (mm(p, hi) + mm(p, mid)) + mm(p, low)
        gram_ref[:, at] = mm3(left_hi[...], left_lo[...], hi, mid)
        return carry

    lax.fori_loop(0, x_ref.shape[1] // NB, share, 0)
    pl.semaphore_wait(barrier, n_row * n_col - 1)

    def chunk(q):
        return pl.ds(q * K, K)

    def core_copy(q):
        return remote(gram_ref.at[ds((1 - core) * half, half), chunk(q)], got_core.at[q], core_send.at[q], core_recv.at[q], sibling)

    def core_back(q):
        piece = full.at[ds(mine, half), chunk(q)]
        return remote(piece, piece, core_send.at[4 + q], core_recv.at[4 + q], sibling)

    def take_core(q):
        core_copy(q).wait()
        acc[q] = gram_ref[ds(mine, half), chunk(q)] + got_core[q]

    def panel_peer(t):
        t = lax.rem(t * 29, 64)
        return row_at(lax.rem(t, 16)), lax.rem(z + t // 16, 4)

    def panel_out(t):
        r, c = panel_peer(t)
        src = acc.at[0, ds(r * 16, 16), ds(c * 128, 128)]
        return remote(src, got_panel.at[t], panel_send.at[0, t], panel_recv.at[0, t], (r, c * 2 + core))

    def panel_back(t):
        r, c = panel_peer(t)
        piece = full.at[ds(mine + row * 16, 16), ds(z * 128, 128)]
        return remote(piece, piece, panel_send.at[1, t], panel_recv.at[1, t], (r, c * 2 + core))

    def loop(lo, hi, act):
        def step(t, carry):
            act(t)
            return carry

        lax.fori_loop(lo, hi, step, 0)

    core_copy(0).start()
    take_core(0)
    loop(1, 64, lambda t: panel_out(t).start())
    for q in (1, 2, 3):
        core_copy(q).start()
    total = acc[0, ds(row * 16, 16), ds(z * 128, 128)]

    def add(t, total):
        panel_out(t).wait()
        return total + got_panel[t]

    total = lax.fori_loop(1, 64, add, total)
    full[ds(mine + row * 16, 16), ds(z * 128, 128)] = total
    loop(1, 64, lambda t: panel_back(t).start())

    def place_of(q):
        first = lax.rem(q + core, 3)
        out = []
        for k in range(3):
            axis = lax.rem(first + k, 3)
            ex, ey, ez = [jnp.where(axis == v, 1, 0) for v in range(3)]
            at = ex * x + ey * y + ez * z

            def peer(d, ex=ex, ey=ey, ez=ez):
                px, py, pz = lax.rem(x + d * ex, 4), lax.rem(y + d * ey, 4), lax.rem(z + d * ez, 4)
                return py * 4 + px, pz * 2 + core

            out.append((at, peer))
        return out

    where = {q: place_of(q) for q in (1, 2, 3)}
    DIST = (1, 2, 3)

    def rest_copies(q, stage_):
        (p1, peer1), (p2, peer2), (p3, peer3) = where[q]
        q1, q2 = half // 4, half // 16
        at1 = p1 * q1
        at2 = at1 + p2 * q2
        copies = []
        for d in DIST:
            slot = stage_ * 3 + d - 1
            sems = rest_send.at[q - 1, slot], rest_recv.at[q - 1, slot]
            if stage_ == 0:
                src, dst, to = acc.at[q, ds(lax.rem(p1 + d, 4) * q1, q1), :], got1.at[q - 1, d - 1], peer1(d)
            elif stage_ == 1:
                src, dst, to = acc.at[q, ds(at1 + lax.rem(p2 + d, 4) * q2, q2), :], got2.at[q - 1, d - 1], peer2(d)
            elif stage_ == 2:
                src = acc.at[q, ds(at2, q2), ds(lax.rem(p3 + d, 4) * 128, 128)]
                dst, to = got3.at[q - 1, d - 1], peer3(d)
            elif stage_ == 3:
                src = dst = full.at[ds(mine + at2, q2), pl.ds(pl.multiple_of(q * K + p3 * 128, 128), 128)]
                to = peer3(d)
            elif stage_ == 4:
                src = dst = full.at[ds(mine + at2, q2), chunk(q)]
                to = peer2(d)
            else:
                src = dst = full.at[ds(mine + at1, q1), chunk(q)]
                to = peer1(d)
            copies.append(remote(src, dst, *sems, to))
        return copies

    def start_rest(stage_):
        for q in (1, 2, 3):
            for copy in rest_copies(q, stage_):
                copy.start()

    def end_rest(stage_):
        for q in (1, 2, 3):
            for copy in rest_copies(q, stage_):
                copy.wait()

    def rest_step(k):
        if k == 0:
            for q in (1, 2, 3):
                take_core(q)
            start_rest(0)
        elif k <= 6:
            end_rest(k - 1)
            q1, q2 = half // 4, half // 16
            for q in (1, 2, 3):
                (p1, _), (p2, _), (p3, _) = where[q]
                at1, at2 = p1 * q1, p1 * q1 + p2 * q2
                if k == 1:
                    acc[q, ds(at1, q1), :] = (acc[q, ds(at1, q1), :] + got1[q - 1, 0]) + (got1[q - 1, 1] + got1[q - 1, 2])
                elif k == 2:
                    acc[q, ds(at2, q2), :] = (acc[q, ds(at2, q2), :] + got2[q - 1, 0]) + (got2[q - 1, 1] + got2[q - 1, 2])
                elif k == 3:
                    last = acc[q, ds(at2, q2), ds(p3 * 128, 128)]
                    full[ds(mine + at2, q2), pl.ds(pl.multiple_of(q * K + p3 * 128, 128), 128)] = (last + got3[q - 1, 0]) + (
                        got3[q - 1, 1] + got3[q - 1, 2]
                    )
            if k < 6:
                start_rest(k)
            else:
                for q in (1, 2, 3):
                    core_back(q).start()
        else:
            for q in (1, 2, 3):
                core_back(q).wait()

    loop(1, 64, lambda t: panel_back(t).wait())
    core_back(0).start()
    rest_step(0)
    core_back(0).wait()

    b = 128
    blocks = K // b
    work[...] = full[:, 0:K]
    cols = lax.broadcasted_iota(jnp.int32, (b, K), 1)
    lines = lax.broadcasted_iota(jnp.int32, (b, K), 0)

    def block(k, carry):
        start = pl.multiple_of(k * b, b)

        def at(k0, step):
            @pl.when(k == k0)
            def _():
                rest_step(step)

        def halfway():
            at(0, 1)
            at(1, 3)
            at(2, 5)
            at(3, 6)

        eliminate(work, top, start, halfway)
        here = (cols >= start) & (cols < start + b)
        line = jnp.where(here, jnp.where(cols - start == lines, 1.0, 0.0), work[pl.ds(start, b), :])
        up = hdot(top[...], line)
        upper[...] = up
        inverse[pl.ds(start, b), :] = jnp.where(cols < start + b, up, 0.0)

        def below(i, c):
            to = pl.multiple_of(i * b, b)
            left = upper[:, pl.ds(to, b)]
            work[pl.ds(to, b), :] = jnp.where(here, 0.0, work[pl.ds(to, b), :]) - hdot(left, upper[...], 0, 0)
            return c

        lax.fori_loop(k + 1, blocks, below, 0)
        at(0, 2)
        at(1, 4)
        return carry

    lax.fori_loop(0, blocks, block, 0)
    hi, lo = split2(inverse[...])
    inv_hi[...], inv_lo[...] = hi, lo
    left_hi, left_lo = split2(rows_ref[:, 0:K])
    q_hi[...], q_lo[...] = split2(mm3(left_hi, left_lo, hi, lo, 1, 1))
    rest_step(7)

    lanes = NB // 2
    arrived = (arrived0, arrived1)

    def message(j, t, h):
        r = row_at(lax.rem(t + 5 * j, 16))
        src = stage.at[j, h, ds(r * per, per), :]
        dst = arrived[h].at[ds(me * per, per), :]
        slot = j * 16 + t
        return remote(src, dst, row_send.at[h, slot], row_recv.at[h, slot], (r, lax.rem(col + j, n_col)))

    def own(h):
        return pltpu.make_async_copy(stage.at[0, h, ds(row * per, per), :], arrived[h].at[ds(me * per, per), :], local_sem.at[h])

    def form(j, carry):
        c = lax.rem(col + j, n_col)
        at = pl.ds(pl.multiple_of(c * NB, NB), NB)
        g_hi, g_lo = split2(full[:, at])
        coef = jnp.concatenate(
            [
                mm3(inv_hi[:NB, :NB], inv_lo[:NB, :NB], g_hi[:NB], g_lo[:NB]),
                mm3(inv_hi[NB:, :], inv_lo[NB:, :], g_hi, g_lo),
            ],
            axis=0,
        )

        @pl.when(j == 0)
        def _():
            coef_ref[...] = coef

        c_hi, c_lo = split2(coef)
        rest = rows_ref[:, at] - mm3(q_hi[...], q_lo[...], c_hi, c_lo)
        stage[j, 0] = rest[:, :lanes]
        stage[j, 1] = rest[:, lanes:]

        @pl.when(j == 0)
        def _():
            own(0).start()
            own(1).start()

        def release(i, carry):
            t = 2 * (j - i) + 1
            message(i, t, 0).start()

            @pl.when(t < 15)
            def _():
                message(i, t + 1, 0).start()

            return carry

        lax.fori_loop(0, j + 1, release, 0)
        return carry

    lax.fori_loop(0, n_col, form, 0)

    def late(t, carry):
        def one(j, carry):
            @pl.when(t + 2 * j > 16)
            def _():
                message(j, t, 0).start()

            return carry

        lax.fori_loop(0, n_col, one, 0)
        return carry

    lax.fori_loop(1, 16, late, 0)
    loop(1, n_col, lambda j: message(j, 0, 0).start())

    def second(t, carry):
        loop(0, n_col, lambda j: message(j, t, 1).start())
        return carry

    lax.fori_loop(1, 16, second, 0)
    loop(1, n_col, lambda j: message(j, 0, 1).start())

    target = target_ref[...]
    n, nodes = target.shape
    mask = jnp.where(target // local_rows == row, 1.0, 0.0)
    before = jnp.where(
        lax.broadcasted_iota(jnp.int32, (nodes, nodes), 0) < lax.broadcasted_iota(jnp.int32, (nodes, nodes), 1), 1.0, 0.0
    ).astype(BF16)
    rank = jnp.where(mask > 0.0, mm(mask.astype(BF16), before), -1.0)
    value = lax.rem(target, local_rows).astype(F32)
    wide = lax.broadcasted_iota(jnp.int32, (n, 128), 1)
    source = lax.broadcasted_iota(jnp.int32, (n, 128), 0)
    for k in range(per):
        spot = jnp.sum(jnp.where(rank == float(k), value, 0.0), axis=1, keepdims=True).astype(jnp.int32)
        number = source * per + k
        low = wide == lax.rem(spot, 128)
        hot_row[pl.ds(k * n, n), :] = jnp.where(wide == spot // 128, 1.0, 0.0).astype(BF16)
        hot_lo[pl.ds(k * n, n), :] = jnp.where(low, lax.rem(number, 64).astype(F32), 0.0).astype(BF16)
        hot_hi[pl.ds(k * n, n), :] = jnp.where(low, (number // 64).astype(F32), 0.0).astype(BF16)
    hot = hot_row[...]
    found = mm(hot, hot_lo[...], 0, 0) + 64.0 * mm(hot, hot_hi[...], 0, 0)
    index[...] = jnp.clip(found[: local_rows // 128, :].astype(jnp.int32), 0, n * per - 1)
    to_smem = pltpu.make_async_copy(index, index_smem, local_sem.at[2])
    to_smem.start()
    to_smem.wait()

    sub = lax.broadcasted_iota(jnp.int32, (8, lanes), 0)
    for h in range(2):
        own(h).wait()

        def arrive(t, carry):
            loop(jnp.where(t == 0, 1, 0), n_col, lambda j: message(j, t, h).wait())
            return carry

        lax.fori_loop(0, 16, arrive, 0)

        def gather(i, carry):
            for u in range(16):
                rows = jnp.broadcast_to(arrived[h][pl.ds(index_smem[i, u * 8], 1), :], (8, lanes))
                for k in range(1, 8):
                    one = jnp.broadcast_to(arrived[h][pl.ds(index_smem[i, u * 8 + k], 1), :], (8, lanes))
                    rows = jnp.where(sub == k, one, rows)
                out_ref[pl.ds(pl.multiple_of(i * 128 + u * 8, 8), 8), pl.ds(h * lanes, lanes)] = rows
            return carry

        lax.fori_loop(0, local_rows // 128, gather, 0)


def finish(snapshots, weight, mine, target, n_row, n_col):
    nodes, snaps = snapshots.shape
    n = n_row * n_col
    local_rows = target.shape[0] // n_row
    per = nodes // n_row
    half = K // 2
    dma = pltpu.SemaphoreType.DMA
    return pl.pallas_call(
        lambda *refs: main_kernel(local_rows, per, *refs),
        out_shape=(jax.ShapeDtypeStruct((K, NB), F32), jax.ShapeDtypeStruct((local_rows, NB), F32)),
        in_specs=[VMEM] * 4,
        out_specs=(VMEM, VMEM),
        scratch_shapes=[
            pltpu.VMEM((nodes, snaps), F32),
            pltpu.VMEM((K, snaps), F32),
            pltpu.VMEM((K, nodes), BF16),
            pltpu.VMEM((K, nodes), BF16),
            pltpu.VMEM((nodes, nodes), BF16),
            pltpu.VMEM((K, snaps), F32),
            pltpu.VMEM((4, half, K), F32),
            pltpu.VMEM((4, half, K), F32),
            pltpu.VMEM((64, 16, 128), F32),
            pltpu.VMEM((3, 3, half // 4, K), F32),
            pltpu.VMEM((3, 3, half // 16, K), F32),
            pltpu.VMEM((3, 3, half // 16, 128), F32),
            pltpu.VMEM((K, K), F32),
            pltpu.VMEM((128, 128), F32),
            pltpu.VMEM((128, K), F32),
            pltpu.VMEM((K, K), F32),
            pltpu.VMEM((K, K), BF16),
            pltpu.VMEM((K, K), BF16),
            pltpu.VMEM((nodes, K), BF16),
            pltpu.VMEM((nodes, K), BF16),
            pltpu.VMEM((n_col, 2, nodes, NB // 2), F32),
            pltpu.VMEM((n * per, NB // 2), F32),
            pltpu.VMEM((n * per, NB // 2), F32),
            pltpu.VMEM((n * per, 128), BF16),
            pltpu.VMEM((n * per, 128), BF16),
            pltpu.VMEM((n * per, 128), BF16),
            pltpu.VMEM((local_rows // 128, 128), jnp.int32),
            pltpu.SMEM((local_rows // 128, 128), jnp.int32),
            dma((8,)),
            dma((8,)),
            dma((2, 64)),
            dma((2, 64)),
            dma((3, 18)),
            dma((3, 18)),
            dma((2, 128)),
            dma((2, 128)),
            dma((3,)),
        ],
        compiler_params=pltpu.CompilerParams(collective_id=1, has_side_effects=True, vmem_limit_bytes=46 << 20),
        name="finish",
    )(snapshots, weight, mine.reshape(1, nodes), target.reshape(n, nodes))


def body(snapshots, district, target):
    n_row, n_col = lax.axis_size("row"), lax.axis_size("col")
    nodes_dev, snaps = snapshots.shape
    me = lax.axis_index(("row", "col"))
    mine = lax.dynamic_slice_in_dim(target, me * nodes_dev, nodes_dev)
    weight = weights_of(district)
    return finish(snapshots, weight, mine, target, n_row, n_col)


def solution(mesh):
    in_specs = (P(("row", "col"), None), P(("row", "col")), P())
    out_specs = (P(None, "col"), P("row", "col"))
    return jax.shard_map(body, mesh=mesh, in_specs=in_specs, out_specs=out_specs, check_vma=False)
```

```python
import jax
import jax.numpy as jnp
from jax import lax
from jax.experimental import pallas as pl
from jax.experimental.pallas import tpu as pltpu
from jax.sharding import PartitionSpec as P

MESH = pl.DeviceIdType.MESH
NB = 256
PANELS = 2
K = PANELS * NB
DIST_MEAN = 256
HIGH = lax.Precision.HIGHEST
F32 = jnp.float32
BF16 = jnp.bfloat16
VMEM = pl.BlockSpec(memory_space=pltpu.VMEM)


def split2(x):
    hi = x.astype(BF16)
    return hi, (x - hi.astype(F32)).astype(BF16)


def dims(a, b):
    return (((a,), (b,)), ((), ()))


def mm(x, y, a=1, b=0):
    return lax.dot_general(x, y, dims(a, b), preferred_element_type=F32)


def mm3(xh, xl, yh, yl, a=1, b=0):
    return mm(xh, yh, a, b) + (mm(xh, yl, a, b) + mm(xl, yh, a, b))


def counts_kernel(district_ref, weight_ref, own, got, send_sem, recv_sem):
    row, col = lax.axis_index("row"), lax.axis_index("col")
    n_row, n_col = lax.axis_size("row"), lax.axis_size("col")
    n = n_row * n_col
    me = row * n_col + col
    steps = (n - 2, n - 1, 1, 2)

    def peer(step):
        other = lax.rem(me + step, n)
        return other // n_col, lax.rem(other, n_col)

    barrier = pltpu.get_barrier_semaphore()
    for step in steps:
        pl.semaphore_signal(barrier, inc=1, device_id=peer(step), device_id_type=MESH)
    nodes = district_ref.shape[0]
    lanes = lax.broadcasted_iota(jnp.int32, (nodes, 256), 1)
    member = district_ref[...] == lanes
    hist = jnp.sum(jnp.where(member, 1.0, 0.0), axis=0, keepdims=True)
    own[...] = jnp.broadcast_to(hist, own.shape)
    pl.semaphore_wait(barrier, 4)
    copies = []
    for k, step in enumerate(steps):
        copy = pltpu.make_async_remote_copy(
            own, got.at[k], send_sem.at[k], recv_sem.at[k], device_id=peer(step), device_id_type=MESH
        )
        copy.start()
        copies.append(copy)
    for copy in copies:
        copy.wait()
    total = own[...]
    valid = (me + 2 < n, me + 1 < n, me >= 1, me >= 2)
    for k in range(4):
        total = total + got[k] * jnp.where(valid[k], 1.0, 0.0)
    scale = jnp.sqrt(DIST_MEAN / jnp.maximum(total, 1.0))[0:1, :]
    weight_ref[...] = jnp.sum(jnp.where(member, scale, 0.0), axis=1, keepdims=True)


def weights_of(district):
    nodes = district.shape[0]
    return pl.pallas_call(
        counts_kernel,
        out_shape=jax.ShapeDtypeStruct((nodes, 1), F32),
        in_specs=[VMEM],
        out_specs=VMEM,
        scratch_shapes=[
            pltpu.VMEM((8, 256), F32),
            pltpu.VMEM((4, 8, 256), F32),
            pltpu.SemaphoreType.DMA((4,)),
            pltpu.SemaphoreType.DMA((4,)),
        ],
        compiler_params=pltpu.CompilerParams(collective_id=0, has_side_effects=True),
        name="counts",
    )(district.reshape(nodes, 1))


def hdot(x, y, a=1, b=0):
    return lax.dot_general(x, y, dims(a, b), precision=HIGH, preferred_element_type=F32)


def eliminate(work, top, start, halfway):
    b=128; groups=b//8
    sub=lax.broadcasted_iota(jnp.int32,(8,b),0); lane=lax.broadcasted_iota(jnp.int32,(8,b),1)
    x=[work[pl.ds(pl.multiple_of(start+8*g,8),8), pl.ds(start,b)] for g in range(groups)]
    for g0 in range(groups):
        if g0 == groups // 2:
            halfway()
        first=8*g0
        column=[[jnp.broadcast_to(x[g][:,first+c:first+c+1],(8,b)) for c in range(8)] for g in range(g0,groups)]
        inside=(lane>=first)&(lane<first+8)
        own=jnp.where(inside,jnp.where(lane-first==sub,1.0,0.0),x[g0])
        y=[jnp.broadcast_to(own[c:c+1,:],(8,b)) for c in range(8)]
        d=[[jnp.broadcast_to(column[0][k][c:c+1,:],(8,b)) for k in range(c+1)] for c in range(8)]
        inv=[]; low=[[None]*8 for _ in range(8)]
        for k in range(8):
            inv.append(1.0/d[k][k])
            for c in range(k+1,8):
                low[c][k]=d[c][k]*inv[k]
            for c in range(k+1,8):
                for m in range(k+1,c+1):
                    d[c][m]=d[c][m]-low[c][k]*d[m][k]
                y[c]=y[c]-low[c][k]*y[k]
        t=jnp.zeros((8,b),F32)
        for c in range(8):
            t=jnp.where(sub==c,y[c]*lax.rsqrt(d[c][c]),t)
        top[pl.ds(first,8),:]=jnp.where(lane<first+8,t,0.0)
        v=[None]*8
        for c in reversed(range(8)):
            a=y[c]*inv[c]
            for k in reversed(range(c+1,8)):
                a=a-low[k][c]*v[k]
            v[c]=a
        for g in range(g0+1,groups):
            m=column[g-g0]
            u=[m[c]*v[c] for c in range(8)]
            s=((u[0]+u[1])+(u[2]+u[3]))+((u[4]+u[5])+(u[6]+u[7]))
            x[g]=jnp.where(inside,0.0,x[g])-s
def main_kernel(local_rows, per, x_hbm, weight_ref, target_ref, coef_ref, out_ref,
                x_ref, rows_ref, gram_ref, left_hi, left_lo, perm, full, got_core, acc, got_panel, got1, got2, got3, work, top, upper, inverse,
                inv_hi, inv_lo, q_hi, q_lo, stage, arrived0, arrived1, hot_row, hot_lo, hot_hi, index, index_smem,
                core_send, core_recv, panel_send, panel_recv, rest_send, rest_recv, row_send, row_recv, local_sem):
    row, col = lax.axis_index("row"), lax.axis_index("col")
    n_row, n_col = lax.axis_size("row"), lax.axis_size("col")
    me = row * n_col + col
    y, x, z, core = row // 4, lax.rem(row, 4), col // 2, lax.rem(col, 2)
    half = K // 2
    sibling = (row, z * 2 + 1 - core)
    mine = core * half

    def ds(start, size):
        return pl.ds(pl.multiple_of(start, size), size)

    def remote(src, dst, send, recv, to):
        return pltpu.make_async_remote_copy(src, dst, send, recv, device_id=to, device_id_type=MESH)

    def row_at(r):
        return lax.rem(y + r // 4, 4) * 4 + lax.rem(x + lax.rem(r, 4), 4)

    bring = pltpu.make_async_copy(x_hbm, x_ref, local_sem.at[3])
    bring.start()

    barrier = pltpu.get_barrier_semaphore()

    def greet(t, carry):
        to = (row_at(lax.rem(t, 16)), lax.rem(col + t // 16, n_col))
        pl.semaphore_signal(barrier, inc=1, device_id=to, device_id_type=MESH)
        return carry

    lax.fori_loop(1, n_row * n_col, greet, 0)
    bring.wait()
    count = x_ref.shape[0]
    weight = jnp.broadcast_to(weight_ref[...], (count, NB))
    for k in range(PANELS):
        hi, lo = split2(x_ref[:, k * NB : (k + 1) * NB] * weight)
        left_hi[k * NB : (k + 1) * NB, :] = hi.T
        left_lo[k * NB : (k + 1) * NB, :] = lo.T
    groups = lax.broadcasted_iota(jnp.int32, (n_row, count), 0)
    belongs = jnp.where(target_ref[pl.ds(me, 1), :] // local_rows == groups, 1.0, 0.0)
    sooner = jnp.where(
        lax.broadcasted_iota(jnp.int32, (count, count), 0) < lax.broadcasted_iota(jnp.int32, (count, count), 1), 1.0, 0.0
    ).astype(BF16)
    spot = mm(belongs.astype(BF16), sooner) + (groups * per).astype(F32)
    spot = jnp.sum(belongs * spot, axis=0, keepdims=True).astype(jnp.int32)
    perm[...] = jnp.where(spot == lax.broadcasted_iota(jnp.int32, (count, count), 0), 1.0, 0.0).astype(BF16)

    def share(i, carry):
        at = pl.ds(pl.multiple_of(i * NB, NB), NB)
        v = x_ref[:, at] * weight
        hi = v.astype(BF16)
        rest = v - hi.astype(F32)
        mid = rest.astype(BF16)
        low = (rest - mid.astype(F32)).astype(BF16)
        p = perm[...]
        rows_ref[:, at] = (mm(p, hi) + mm(p, mid)) + mm(p, low)
        gram_ref[:, at] = mm3(left_hi[...], left_lo[...], hi, mid)
        return carry

    lax.fori_loop(0, x_ref.shape[1] // NB, share, 0)
    pl.semaphore_wait(barrier, n_row * n_col - 1)

    def chunk(q):
        return pl.ds(q * K, K)

    def core_copy(q):
        return remote(gram_ref.at[ds((1 - core) * half, half), chunk(q)], got_core.at[q], core_send.at[q], core_recv.at[q], sibling)

    def core_back(q):
        piece = full.at[ds(mine, half), chunk(q)]
        return remote(piece, piece, core_send.at[4 + q], core_recv.at[4 + q], sibling)

    def take_core(q):
        core_copy(q).wait()
        acc[q] = gram_ref[ds(mine, half), chunk(q)] + got_core[q]

    def panel_peer(t):
        t = lax.rem(t * 29, 64)
        return row_at(lax.rem(t, 16)), lax.rem(z + t // 16, 4)

    def panel_out(t):
        r, c = panel_peer(t)
        src = acc.at[0, ds(r * 16, 16), ds(c * 128, 128)]
        return remote(src, got_panel.at[t], panel_send.at[0, t], panel_recv.at[0, t], (r, c * 2 + core))

    def panel_back(t):
        r, c = panel_peer(t)
        piece = full.at[ds(mine + row * 16, 16), ds(z * 128, 128)]
        return remote(piece, piece, panel_send.at[1, t], panel_recv.at[1, t], (r, c * 2 + core))

    def loop(lo, hi, act):
        def step(t, carry):
            act(t)
            return carry

        lax.fori_loop(lo, hi, step, 0)

    core_copy(0).start()
    take_core(0)
    loop(1, 64, lambda t: panel_out(t).start())
    for q in (1, 2, 3):
        core_copy(q).start()
    total = acc[0, ds(row * 16, 16), ds(z * 128, 128)]

    def add(t, total):
        panel_out(t).wait()
        return total + got_panel[t]

    total = lax.fori_loop(1, 64, add, total)
    full[ds(mine + row * 16, 16), ds(z * 128, 128)] = total
    loop(1, 64, lambda t: panel_back(t).start())

    def place_of(q):
        first = lax.rem(q + core, 3)
        out = []
        for k in range(3):
            axis = lax.rem(first + k, 3)
            ex, ey, ez = [jnp.where(axis == v, 1, 0) for v in range(3)]
            at = ex * x + ey * y + ez * z

            def peer(d, ex=ex, ey=ey, ez=ez):
                px, py, pz = lax.rem(x + d * ex, 4), lax.rem(y + d * ey, 4), lax.rem(z + d * ez, 4)
                return py * 4 + px, pz * 2 + core

            out.append((at, peer))
        return out

    where = {q: place_of(q) for q in (1, 2, 3)}
    DIST = (1, 2, 3)

    def rest_copies(q, stage_):
        (p1, peer1), (p2, peer2), (p3, peer3) = where[q]
        q1, q2 = half // 4, half // 16
        at1 = p1 * q1
        at2 = at1 + p2 * q2
        copies = []
        for d in DIST:
            slot = stage_ * 3 + d - 1
            sems = rest_send.at[q - 1, slot], rest_recv.at[q - 1, slot]
            if stage_ == 0:
                src, dst, to = acc.at[q, ds(lax.rem(p1 + d, 4) * q1, q1), :], got1.at[q - 1, d - 1], peer1(d)
            elif stage_ == 1:
                src, dst, to = acc.at[q, ds(at1 + lax.rem(p2 + d, 4) * q2, q2), :], got2.at[q - 1, d - 1], peer2(d)
            elif stage_ == 2:
                src = acc.at[q, ds(at2, q2), ds(lax.rem(p3 + d, 4) * 128, 128)]
                dst, to = got3.at[q - 1, d - 1], peer3(d)
            elif stage_ == 3:
                src = dst = full.at[ds(mine + at2, q2), pl.ds(pl.multiple_of(q * K + p3 * 128, 128), 128)]
                to = peer3(d)
            elif stage_ == 4:
                src = dst = full.at[ds(mine + at2, q2), chunk(q)]
                to = peer2(d)
            else:
                src = dst = full.at[ds(mine + at1, q1), chunk(q)]
                to = peer1(d)
            copies.append(remote(src, dst, *sems, to))
        return copies

    def start_rest(stage_):
        for q in (1, 2, 3):
            for copy in rest_copies(q, stage_):
                copy.start()

    def end_rest(stage_):
        for q in (1, 2, 3):
            for copy in rest_copies(q, stage_):
                copy.wait()

    def rest_step(k):
        if k == 0:
            for q in (1, 2, 3):
                take_core(q)
            start_rest(0)
        elif k <= 6:
            end_rest(k - 1)
            q1, q2 = half // 4, half // 16
            for q in (1, 2, 3):
                (p1, _), (p2, _), (p3, _) = where[q]
                at1, at2 = p1 * q1, p1 * q1 + p2 * q2
                if k == 1:
                    acc[q, ds(at1, q1), :] = (acc[q, ds(at1, q1), :] + got1[q - 1, 0]) + (got1[q - 1, 1] + got1[q - 1, 2])
                elif k == 2:
                    acc[q, ds(at2, q2), :] = (acc[q, ds(at2, q2), :] + got2[q - 1, 0]) + (got2[q - 1, 1] + got2[q - 1, 2])
                elif k == 3:
                    last = acc[q, ds(at2, q2), ds(p3 * 128, 128)]
                    full[ds(mine + at2, q2), pl.ds(pl.multiple_of(q * K + p3 * 128, 128), 128)] = (last + got3[q - 1, 0]) + (
                        got3[q - 1, 1] + got3[q - 1, 2]
                    )
            if k < 6:
                start_rest(k)
            else:
                for q in (1, 2, 3):
                    core_back(q).start()
        else:
            for q in (1, 2, 3):
                core_back(q).wait()

    loop(1, 64, lambda t: panel_back(t).wait())
    core_back(0).start()
    rest_step(0)
    core_back(0).wait()

    b = 128
    blocks = K // b
    work[...] = full[:, 0:K]
    cols = lax.broadcasted_iota(jnp.int32, (b, K), 1)
    lines = lax.broadcasted_iota(jnp.int32, (b, K), 0)

    def block(k, carry):
        start = pl.multiple_of(k * b, b)

        def at(k0, step):
            @pl.when(k == k0)
            def _():
                rest_step(step)

        def halfway():
            at(0, 1)
            at(1, 3)
            at(2, 5)
            at(3, 6)

        eliminate(work, top, start, halfway)
        here = (cols >= start) & (cols < start + b)
        line = jnp.where(here, jnp.where(cols - start == lines, 1.0, 0.0), work[pl.ds(start, b), :])
        up = hdot(top[...], line)
        upper[...] = up
        inverse[pl.ds(start, b), :] = jnp.where(cols < start + b, up, 0.0)

        def below(i, c):
            to = pl.multiple_of(i * b, b)
            left = upper[:, pl.ds(to, b)]
            work[pl.ds(to, b), :] = jnp.where(here, 0.0, work[pl.ds(to, b), :]) - hdot(left, upper[...], 0, 0)
            return c

        lax.fori_loop(k + 1, blocks, below, 0)
        at(0, 2)
        at(1, 4)
        return carry

    lax.fori_loop(0, blocks, block, 0)
    hi, lo = split2(inverse[...])
    inv_hi[...], inv_lo[...] = hi, lo
    left_hi, left_lo = split2(rows_ref[:, 0:K])
    q_hi[...], q_lo[...] = split2(mm3(left_hi, left_lo, hi, lo, 1, 1))
    rest_step(7)

    lanes = NB // 2
    arrived = (arrived0, arrived1)

    def message(j, t, h):
        r = row_at(lax.rem(t + 5 * j, 16))
        src = stage.at[j, h, ds(r * per, per), :]
        dst = arrived[h].at[ds(me * per, per), :]
        slot = j * 16 + t
        return remote(src, dst, row_send.at[h, slot], row_recv.at[h, slot], (r, lax.rem(col + j, n_col)))

    def own(h):
        return pltpu.make_async_copy(stage.at[0, h, ds(row * per, per), :], arrived[h].at[ds(me * per, per), :], local_sem.at[h])

    def form(j, carry):
        c = lax.rem(col + j, n_col)
        at = pl.ds(pl.multiple_of(c * NB, NB), NB)
        g_hi, g_lo = split2(full[:, at])
        coef = jnp.concatenate(
            [
                mm3(inv_hi[:NB, :NB], inv_lo[:NB, :NB], g_hi[:NB], g_lo[:NB]),
                mm3(inv_hi[NB:, :], inv_lo[NB:, :], g_hi, g_lo),
            ],
            axis=0,
        )

        @pl.when(j == 0)
        def _():
            coef_ref[...] = coef

        c_hi, c_lo = split2(coef)
        rest = rows_ref[:, at] - mm3(q_hi[...], q_lo[...], c_hi, c_lo)
        stage[j, 0] = rest[:, :lanes]
        stage[j, 1] = rest[:, lanes:]

        @pl.when(j == 0)
        def _():
            own(0).start()
            own(1).start()

        def release(i, carry):
            for u in range(4):
                t = 4 * (j - i) + 1 + u

                @pl.when(t < 16)
                def _(t=t):
                    message(i, t, 0).start()

            return carry

        lax.fori_loop(0, j + 1, release, 0)
        return carry

    lax.fori_loop(0, n_col, form, 0)

    def late(t, carry):
        def one(j, carry):
            @pl.when(t + 4 * j > 32)
            def _():
                message(j, t, 0).start()

            return carry

        lax.fori_loop(0, n_col, one, 0)
        return carry

    lax.fori_loop(1, 16, late, 0)
    loop(1, n_col, lambda j: message(j, 0, 0).start())

    def second(t, carry):
        loop(0, n_col, lambda j: message(j, t, 1).start())
        return carry

    lax.fori_loop(1, 16, second, 0)
    loop(1, n_col, lambda j: message(j, 0, 1).start())

    target = target_ref[...]
    n, nodes = target.shape
    mask = jnp.where(target // local_rows == row, 1.0, 0.0)
    before = jnp.where(
        lax.broadcasted_iota(jnp.int32, (nodes, nodes), 0) < lax.broadcasted_iota(jnp.int32, (nodes, nodes), 1), 1.0, 0.0
    ).astype(BF16)
    rank = jnp.where(mask > 0.0, mm(mask.astype(BF16), before), -1.0)
    value = lax.rem(target, local_rows).astype(F32)
    wide = lax.broadcasted_iota(jnp.int32, (n, 128), 1)
    source = lax.broadcasted_iota(jnp.int32, (n, 128), 0)
    for k in range(per):
        spot = jnp.sum(jnp.where(rank == float(k), value, 0.0), axis=1, keepdims=True).astype(jnp.int32)
        number = source * per + k
        low = wide == lax.rem(spot, 128)
        hot_row[pl.ds(k * n, n), :] = jnp.where(wide == spot // 128, 1.0, 0.0).astype(BF16)
        hot_lo[pl.ds(k * n, n), :] = jnp.where(low, lax.rem(number, 64).astype(F32), 0.0).astype(BF16)
        hot_hi[pl.ds(k * n, n), :] = jnp.where(low, (number // 64).astype(F32), 0.0).astype(BF16)
    hot = hot_row[...]
    found = mm(hot, hot_lo[...], 0, 0) + 64.0 * mm(hot, hot_hi[...], 0, 0)
    index[...] = jnp.clip(found[: local_rows // 128, :].astype(jnp.int32), 0, n * per - 1)
    to_smem = pltpu.make_async_copy(index, index_smem, local_sem.at[2])
    to_smem.start()
    to_smem.wait()

    sub = lax.broadcasted_iota(jnp.int32, (8, lanes), 0)
    for h in range(2):
        own(h).wait()

        def arrive(t, carry):
            loop(jnp.where(t == 0, 1, 0), n_col, lambda j: message(j, t, h).wait())
            return carry

        lax.fori_loop(0, 16, arrive, 0)

        def gather(i, carry):
            for u in range(16):
                rows = jnp.broadcast_to(arrived[h][pl.ds(index_smem[i, u * 8], 1), :], (8, lanes))
                for k in range(1, 8):
                    one = jnp.broadcast_to(arrived[h][pl.ds(index_smem[i, u * 8 + k], 1), :], (8, lanes))
                    rows = jnp.where(sub == k, one, rows)
                out_ref[pl.ds(pl.multiple_of(i * 128 + u * 8, 8), 8), pl.ds(h * lanes, lanes)] = rows
            return carry

        lax.fori_loop(0, local_rows // 128, gather, 0)


def finish(snapshots, weight, target, n_row, n_col):
    nodes, snaps = snapshots.shape
    n = n_row * n_col
    local_rows = target.shape[0] // n_row
    per = nodes // n_row
    half = K // 2
    dma = pltpu.SemaphoreType.DMA
    return pl.pallas_call(
        lambda *refs: main_kernel(local_rows, per, *refs),
        out_shape=(jax.ShapeDtypeStruct((K, NB), F32), jax.ShapeDtypeStruct((local_rows, NB), F32)),
        in_specs=[pl.BlockSpec(memory_space=pl.ANY), VMEM, VMEM],
        out_specs=(VMEM, VMEM),
        scratch_shapes=[
            pltpu.VMEM((nodes, snaps), F32),
            pltpu.VMEM((nodes, snaps), F32),
            pltpu.VMEM((K, snaps), F32),
            pltpu.VMEM((K, nodes), BF16),
            pltpu.VMEM((K, nodes), BF16),
            pltpu.VMEM((nodes, nodes), BF16),
            pltpu.VMEM((K, snaps), F32),
            pltpu.VMEM((4, half, K), F32),
            pltpu.VMEM((4, half, K), F32),
            pltpu.VMEM((64, 16, 128), F32),
            pltpu.VMEM((3, 3, half // 4, K), F32),
            pltpu.VMEM((3, 3, half // 16, K), F32),
            pltpu.VMEM((3, 3, half // 16, 128), F32),
            pltpu.VMEM((K, K), F32),
            pltpu.VMEM((128, 128), F32),
            pltpu.VMEM((128, K), F32),
            pltpu.VMEM((K, K), F32),
            pltpu.VMEM((K, K), BF16),
            pltpu.VMEM((K, K), BF16),
            pltpu.VMEM((nodes, K), BF16),
            pltpu.VMEM((nodes, K), BF16),
            pltpu.VMEM((n_col, 2, nodes, NB // 2), F32),
            pltpu.VMEM((n * per, NB // 2), F32),
            pltpu.VMEM((n * per, NB // 2), F32),
            pltpu.VMEM((n * per, 128), BF16),
            pltpu.VMEM((n * per, 128), BF16),
            pltpu.VMEM((n * per, 128), BF16),
            pltpu.VMEM((local_rows // 128, 128), jnp.int32),
            pltpu.SMEM((local_rows // 128, 128), jnp.int32),
            dma((8,)),
            dma((8,)),
            dma((2, 64)),
            dma((2, 64)),
            dma((3, 18)),
            dma((3, 18)),
            dma((2, 128)),
            dma((2, 128)),
            dma((4,)),
        ],
        compiler_params=pltpu.CompilerParams(collective_id=1, has_side_effects=True, vmem_limit_bytes=46 << 20),
        name="finish",
    )(snapshots, weight, target.reshape(n, nodes))


def body(snapshots, district, target):
    n_row, n_col = lax.axis_size("row"), lax.axis_size("col")
    weight = weights_of(district)
    return finish(snapshots, weight, target, n_row, n_col)


def solution(mesh):
    in_specs = (P(("row", "col"), None), P(("row", "col")), P())
    out_specs = (P(None, "col"), P("row", "col"))
    return jax.shard_map(body, mesh=mesh, in_specs=in_specs, out_specs=out_specs, check_vma=False)
```
